256 devices in a mesh: px: 32 (over z, x), py: 8 (over y, core).
Axes of the slice: x: 4, y: 4, z: 8, core: 2. Of those that a mesh axis runs over, the one named last changes fastest.
Arguments:
- counts: int32 [32], replicated, may hold values from 1 to 6, 64 in all
- coefficient: float32 [192, 8, 4096], P('px', 'py'), may hold values from 0.2 to 5
- signs: int32 [192, 8, 4096], P('px', 'py'), may hold values from 0 to 1
- basis_old: float32 [192, 8, 16, 4096], P('px', 'py'), may hold values from -8 to 8
- basis_last: float32 [192, 8, 16, 4096], P('px', 'py'), may hold values from -8 to 8
- residual_factor: float32 [16, 16], replicated, may hold values from -12 to 12
- previous_coef: float32 [32, 16], replicated, may hold values from -12 to 12
- sample_rows: int32 [2048], replicated, may hold values from 0 to 2097151, as said below
Outputs:
- new_block: float32 [192, 8, 16, 4096], P('px', 'py')
- sketch: float32 [48, 2048], P(None, ('px', 'py'))
- solution: float32 [32, 16], replicated
The draws below stay inside these ranges and needn't reach their ends.
Inputs may be any that keep to these rules, and one draw needn't show every extreme that they name: Index i of px owns counts[i] consecutive patch columns, in px order; the largest count is exactly 6. `sample_rows`: distinct cell numbers, among them 0 and 2097151.
All inputs are finite; a program needn't handle non-finite values.
Results may differ from the reference program's by a relative error of at most 0.0003.
Values sent between devices are 32-bit elements; how exact they have to be, the bound alone decides.
No kernel may reach another device: no remote copies, remote signals or barrier semaphores. Data moves between devices by JAX's collectives and lax.ppermute only.
A program may use at most 256 MiB of HBM per device.

```python
import math
import jax
import jax.numpy as jnp
import numpy as np
from jax import lax

PS = 16
RHS = 16
K = 2048
MEANX = 2
CAP = 6
CELLS = 4096
GX = 64
NPATCH = 512
NC = 2097152
N_PX = 32
N_PY = 8


def basis_pair(key):
    shape_all = (N_PX * CAP, N_PY, RHS, CELLS)
    fresh_old = jax.random.normal(jax.random.fold_in(key, 11), shape_all, jnp.float32)
    fresh_last = jax.random.normal(jax.random.fold_in(key, 12), shape_all, jnp.float32)
    mixing = jax.random.normal(jax.random.fold_in(key, 13), (RHS, RHS), jnp.float32) / math.sqrt(RHS)
    mixed = jnp.einsum('sygc,gh->syhc', fresh_last, mixing)
    older = 0.6 * mixed + 0.8 * fresh_old
    return (jnp.clip(older, -8.0, 8.0), jnp.clip(fresh_last, -8.0, 8.0))


def draw_basis_old(key, part):
    return basis_pair(key)[0]


def draw_basis_last(key, part):
    return basis_pair(key)[1]


def draw_previous_coef(key, part):
    noise = jnp.clip(jax.random.normal(jax.random.fold_in(key, 32), (2 * RHS, RHS), jnp.float32), -4.0, 4.0)
    leading = jnp.concatenate([6.0 * jnp.eye(RHS, dtype=jnp.float32), jnp.zeros((RHS, RHS), jnp.float32)], axis=0)
    return jnp.clip(leading + noise, -12.0, 12.0)


def draw_sample_rows(key, part):
    middle = jax.random.permutation(jax.random.fold_in(key, 21), NC - 2)[:K - 2].astype(jnp.int32) + 1
    chosen = jnp.concatenate([jnp.array([0, NC - 1], jnp.int32), middle])
    shuffle_idx = jax.random.permutation(jax.random.fold_in(key, 22), K)
    return chosen[shuffle_idx].astype(jnp.int32)


def touch_ends(values, own_key, low, top_value):
    dims = values.shape
    place = [jax.random.randint(jax.random.fold_in(own_key, axis), (), 0, dims[axis]) for axis in range(len(dims))]
    values = values.at[tuple(place)].set(low)
    longest = dims.index(max(dims))
    place[longest] = (place[longest] + 1) % dims[longest]
    return values.at[tuple(place)].set(top_value)


def steps_of(stream_key, shape, cuts, low, high):
    level = 1.0
    for position, blocks in cuts:
        steps = jax.random.uniform(jax.random.fold_in(jax.random.fold_in(stream_key, 6), position), (blocks,), jnp.float32, low / len(cuts), high / len(cuts))
        level = level * jnp.repeat(jnp.exp(steps), shape[position] // blocks).reshape((-1,) + (1,) * (len(shape) - 1 - position))
    return level


def length_profile(count, total, limit, skew):
    portions = [(1 << 20) // math.isqrt(grade ** skew) + 1 for grade in range(2, count + 1)]
    spare, holding = total - limit - (count - 1), [1] * (count - 1)
    while spare > 0:
        candidates = [i for i in range(count - 1) if holding[i] < limit]
        pool, budget = sum([portions[i] for i in candidates]), spare
        for i in candidates:
            extra = min(limit - holding[i], max(1, budget * portions[i] // pool), spare)
            holding[i] = holding[i] + extra
            spare = spare - extra
    return np.array([limit] + holding)


def uneven(own_key, count, total, reach, skew):
    if count == 2:
        one = jax.random.randint(own_key, (), max(1, total - reach), min(reach, total - 1) + 1)
        return jnp.stack([one, total - one])
    sizes = jnp.asarray(length_profile(count, total, reach, skew), jnp.int32)
    twos = (count - 1) // 2
    source_of, receiver = sizes[1:1 + 2 * twos:2], sizes[2:2 + 2 * twos:2]
    slack = jnp.minimum(source_of - 1, reach - receiver)
    passed = jax.random.randint(jax.random.fold_in(own_key, 1), (twos,), 0, 1 << 20) % (slack + 1)
    sizes = sizes.at[1:1 + 2 * twos:2].set(source_of - passed).at[2:2 + 2 * twos:2].set(receiver + passed)
    return sizes[jax.random.permutation(jax.random.fold_in(own_key, 2), count)]


def centred(own_key, dims, scale, bound, kind=jnp.bfloat16):
    drawn = scale * jax.random.normal(own_key, dims, jnp.float32)
    return jnp.clip(drawn, min=-bound, max=bound).astype(kind)


def setup_inputs(seed: int = 0) -> dict:
    arg_keys = jax.random.split(jax.random.key(seed), 9)
    counts = uneven(arg_keys[0], N_PX, MEANX * N_PX, 3 * MEANX, 2).astype(jnp.int32)
    coefficient = jnp.clip(jnp.exp(math.log(5.0) - 3.218876 * jax.random.uniform(arg_keys[1], (N_PX * CAP, N_PY, CELLS), jnp.float32) ** steps_of(arg_keys[1], (N_PX * CAP, N_PY, CELLS), ((0, 32), (1, 8)), -0.2, 0.2)), 0.2, 5.0)
    signs = touch_ends(jax.random.randint(arg_keys[2], (N_PX * CAP, N_PY, CELLS), 0, 2), jax.random.fold_in(arg_keys[2], 1), 0, 1).astype(jnp.int32)
    basis_old = draw_basis_old(jax.random.fold_in(arg_keys[8], 71), 0)
    basis_last = draw_basis_last(jax.random.fold_in(arg_keys[8], 71), 0)
    residual_factor = centred(arg_keys[5], (RHS, RHS), 3.0, 12.0, jnp.float32)
    previous_coef = draw_previous_coef(jax.random.fold_in(arg_keys[8], 71), 0)
    sample_rows = draw_sample_rows(jax.random.fold_in(arg_keys[8], 71), 0)
    return dict(counts=counts, coefficient=coefficient, signs=signs, basis_old=basis_old, basis_last=basis_last, residual_factor=residual_factor, previous_coef=previous_coef, sample_rows=sample_rows)


highest = lax.Precision.HIGHEST

def parity_of(values):
    folded = values
    for amount in (16, 8, 4, 2, 1):
        folded = jnp.bitwise_xor(folded, jnp.right_shift(folded, amount))
    return jnp.bitwise_and(folded, 1)

def sign_table(length):
    indices = jnp.arange(length, dtype=jnp.int32)
    parity = parity_of(jnp.bitwise_and(indices[:, None], indices[None, :]))
    return (1 - 2 * parity).astype(jnp.float32)

def transform_cells(values):
    inner_len = min(CELLS, 128)
    outer_len = CELLS // inner_len
    shaped = values.reshape(values.shape[:-1] + (outer_len, inner_len))
    shaped = jnp.einsum('sjab,bd->sjad', shaped, sign_table(inner_len), precision=highest)
    shaped = jnp.einsum('ca,sjad->sjcd', sign_table(outer_len), shaped, precision=highest)
    return shaped.reshape(values.shape)

def patch_slots(counts):
    offsets = jnp.cumsum(counts) - counts
    ends = offsets + counts
    column_ids = jnp.arange(GX, dtype=jnp.int32)
    owner_ids = lax.optimization_barrier(jnp.sum((column_ids[:, None] >= ends[None, :]).astype(jnp.int32), axis=1)).astype(jnp.int32)
    return (owner_ids * CAP + column_ids - offsets[owner_ids]).astype(jnp.int32)

def to_grid(field_vals):
    channels = field_vals.shape[2]
    cube_vals = field_vals.reshape(GX, N_PY, channels, PS, PS, PS)
    return jnp.transpose(cube_vals, (2, 0, 3, 1, 4, 5)).reshape(channels, GX * PS, N_PY * PS, PS)

def from_grid(grid_vals):
    channels = grid_vals.shape[0]
    cube_vals = grid_vals.reshape(channels, GX, PS, N_PY, PS, PS)
    return jnp.transpose(cube_vals, (1, 3, 0, 2, 4, 5)).reshape(GX, N_PY, channels, CELLS)

def operate_one(values, kappa_grid):
    padded = jnp.pad(values, 1)
    kappa_pad = jnp.pad(kappa_grid, 1)
    extents = values.shape
    summed = jnp.zeros_like(values)
    for movement in ((1, 0, 0), (-1, 0, 0), (0, 1, 0), (0, -1, 0), (0, 0, 1), (0, 0, -1)):
        starts = tuple((1 + movement[dim_idx] for dim_idx in range(3)))
        limits = tuple((starts[dim_idx] + extents[dim_idx] for dim_idx in range(3)))
        neighbour_vals = lax.slice(padded, starts, limits)
        neighbour_kappa = lax.slice(kappa_pad, starts, limits)
        summed = summed + 0.5 * (kappa_grid + neighbour_kappa) * (values - neighbour_vals)
    return summed

def sketch_rows(field_vals, sign_flips, sample_rows):
    columns = (field_vals * sign_flips[:, :, None, :]).reshape(NPATCH, field_vals.shape[2], CELLS)
    spread = transform_cells(columns)
    patch_ids = jnp.arange(NPATCH, dtype=jnp.int32)
    block_len = min(K, 512)
    row_blocks = sample_rows.reshape(K // block_len, block_len)

    def one_block(block_rows):
        picked = jnp.take(spread, block_rows % CELLS, axis=2)
        parity = parity_of(jnp.bitwise_and(patch_ids[:, None], (block_rows // CELLS)[None, :]))
        weights = (1 - 2 * parity).astype(jnp.float32)
        return jnp.einsum('pk,pjk->jk', weights, picked, precision=highest)
    pieces = lax.map(one_block, row_blocks)
    joined = jnp.transpose(pieces, (1, 0, 2)).reshape(field_vals.shape[2], K)
    return joined * (1.0 / math.sqrt(NC))

def normal_parts(sketch_cols, proj_coef, previous_coef, residual_factor):
    pair_count = proj_coef.shape[0]
    width_rhs = proj_coef.shape[1]
    pair_rows = sketch_cols[:pair_count]
    first_image = jnp.einsum('ab,ak->bk', previous_coef, pair_rows, precision=highest)
    second_image = jnp.einsum('ab,ak->bk', proj_coef, pair_rows, precision=highest) + sketch_cols[pair_count:]
    images = jnp.concatenate([first_image, second_image], axis=0)
    target = jnp.einsum('ab,ak->bk', residual_factor, sketch_cols[:width_rhs], precision=highest)
    return (jnp.dot(images, images.T, precision=highest), jnp.dot(images, target.T, precision=highest))

def solve_normal(normal_gram, normal_cross):
    factor_low = jnp.linalg.cholesky(normal_gram)
    middle = lax.linalg.triangular_solve(factor_low, normal_cross, left_side=True, lower=True)
    return lax.linalg.triangular_solve(factor_low, middle, left_side=True, lower=True, transpose_a=True)

def reference(counts, coefficient, signs, basis_old, basis_last, residual_factor, previous_coef, sample_rows):
    slot_ids = patch_slots(counts)
    old_glob = basis_old[slot_ids]
    last_glob = basis_last[slot_ids]
    kappa_glob = coefficient[slot_ids]
    sign_flips = (1 - 2 * signs[slot_ids]).astype(jnp.float32)
    kappa_grid = to_grid(kappa_glob[:, :, None, :])[0]
    image = from_grid(lax.map(lambda values: operate_one(values, kappa_grid), to_grid(last_glob)))
    pair = jnp.concatenate([old_glob, last_glob], axis=2)
    proj_coef = jnp.einsum('pyac,pybc->ab', pair, image, precision=highest) / NC
    newer = image - jnp.einsum('pyac,ab->pybc', pair, proj_coef, precision=highest)
    sketch = jnp.concatenate([sketch_rows(old_glob, sign_flips, sample_rows), sketch_rows(last_glob, sign_flips, sample_rows), sketch_rows(newer, sign_flips, sample_rows)], axis=0)
    normal_gram, normal_cross = normal_parts(sketch, proj_coef, previous_coef, residual_factor)
    solution = solve_normal(normal_gram, normal_cross)
    new_block = jnp.zeros((N_PX * CAP, N_PY, RHS, CELLS), jnp.float32).at[slot_ids].set(newer)
    return (new_block, sketch, solution)
```

```python
import functools
import math

import jax
import jax.numpy as jnp
from jax import lax
from jax.experimental import pallas as pl
from jax.experimental.pallas import tpu as pltpu
from jax.sharding import PartitionSpec as P

PS = 16
RHS = 16
K = 2048
CAP = 6
CELLS = 4096
NC = 2097152
FACE = PS * PS
LANES = 128
N_PX = 32
N_PY = 8
N_Z = 8
GROUP = 32
SHARE = K // (N_PX * N_PY)
AXES = ("px", "py")

F32 = jnp.float32
BF16 = jnp.bfloat16
highest = lax.Precision.HIGHEST


def iota(shape, dim):
    return lax.broadcasted_iota(jnp.int32, shape, dim)


def sign_of(bits):
    for amount in (8, 4, 2, 1):
        bits = bits ^ (bits >> amount)
    return (1 - 2 * (bits & 1)).astype(F32)


def split(values):
    high = values.astype(BF16)
    return high, (values - high.astype(F32)).astype(BF16)


def lane_roll(tile, shift):
    shift = shift % LANES
    return pltpu.roll(tile, shift, 1) if shift else tile


def held_of(counts_ref):
    return counts_ref[lax.axis_index("px")]


def offset_of(counts_ref):
    index = lax.axis_index("px")
    return lax.fori_loop(
        0, N_PX, lambda i, total: total + jnp.where(i < index, counts_ref[i], 0), jnp.int32(0)
    )


def pack_kernel(counts_ref, last_ref, coef_ref, xlo_ref, xhi_ref, ylo_ref, yhi_ref, kap_ref):
    held = held_of(counts_ref)
    kap_ref[...] = jnp.zeros_like(kap_ref)
    for slot in range(CAP):
        kap_ref[slot : slot + 1, :] = coef_ref[slot]
    xlo_ref[0:RHS, :] = last_ref[0, 0, :, 0:FACE]
    xlo_ref[RHS : RHS + 8, :] = jnp.broadcast_to(kap_ref[0:1, 0:FACE], (8, FACE))
    xhi_ref[0:RHS, :] = last_ref[held - 1, 0, :, CELLS - FACE : CELLS]
    xhi_ref[RHS : RHS + 8, :] = jnp.broadcast_to(
        coef_ref[held - 1, :, CELLS - FACE : CELLS], (8, FACE)
    )
    run = iota((8, LANES), 1) // PS

    def faces(read, row):
        for col in range(2):
            low = jnp.zeros((8, LANES), F32)
            high = jnp.zeros((8, LANES), F32)
            for step in range(8):
                plane = col * 8 + step
                low = jnp.where(run == step, lane_roll(read(2 * plane), PS * step), low)
                high = jnp.where(run == step, lane_roll(read(2 * plane + 1), PS * step + PS), high)
            ylo_ref[pl.ds(row, 8), col * LANES : (col + 1) * LANES] = low
            yhi_ref[pl.ds(row, 8), col * LANES : (col + 1) * LANES] = high

    def one_slot(slot, carry):
        for half in range(2):
            faces(
                lambda j: last_ref[slot, 0, 8 * half : 8 * half + 8, j * LANES : (j + 1) * LANES],
                pl.multiple_of(slot * RHS + 8 * half, 8),
            )
        return carry

    lax.fori_loop(0, CAP, one_slot, 0)
    faces(lambda j: kap_ref[:, j * LANES : (j + 1) * LANES], CAP * RHS)


def add_sketch(high_ref, low_ref, table_ref, weight_ref, out_ref, rows):
    out_ref[...] = jnp.zeros_like(out_ref)

    def one_slot(slot, carry):
        at = pl.ds(pl.multiple_of(slot * PS * rows, 16), PS * rows)
        high = high_ref[at, :]
        low = low_ref[at, :]
        for block in range(K // 256):
            lanes = slice(block * 256, (block + 1) * 256)
            table = table_ref[:, lanes]
            mixed = jnp.dot(high, table, preferred_element_type=F32) + jnp.dot(
                low, table, preferred_element_type=F32
            )
            weight = weight_ref[pl.ds(pl.multiple_of(slot * PS, 16), PS), lanes]
            total = out_ref[:, lanes]
            for plane in range(PS):
                total = total + weight[plane : plane + 1] * mixed[plane * rows : (plane + 1) * rows]
            out_ref[:, lanes] = total
        return carry

    lax.fori_loop(0, CAP, one_slot, 0)


def pair_kernel(
    counts_ref, rows_ref, old_ref, last_ref, signs_ref,
    table_ref, weight_ref, high_ref, low_ref, part_ref,
):
    held = held_of(counts_ref)
    offset = offset_of(counts_ref)
    rows = rows_ref[...]
    index = iota((16, K), 0)
    inner = sign_of(index & (rows & 15))
    outer = sign_of(index & ((rows >> 4) & 15))
    for step in range(16):
        table_ref[16 * step : 16 * step + 16, :] = (inner * outer[step : step + 1]).astype(BF16)
    plane_sign = sign_of(index & ((rows >> 8) & 15))
    slot_ids = iota((8, K), 0)
    patch = (offset + slot_ids) * N_PY + lax.axis_index("py")
    slot_sign = sign_of(patch & (rows >> 12)) * jnp.where(
        slot_ids < held, 1.0 / math.sqrt(NC), 0.0
    )
    for slot in range(CAP):
        weight_ref[slot * PS : (slot + 1) * PS, :] = plane_sign * slot_sign[slot : slot + 1]

    def prepare(slot, carry):
        flips = (1 - 2 * signs_ref[slot]).astype(F32)
        for place, ref in ((0, old_ref), (1, last_ref)):
            high, low = split(ref[slot, 0] * flips)
            for plane in range(PS):
                at = pl.ds(pl.multiple_of((slot * PS + plane) * 32 + 16 * place, 16), 16)
                high_ref[at, :] = high[:, plane * FACE : (plane + 1) * FACE]
                low_ref[at, :] = low[:, plane * FACE : (plane + 1) * FACE]
        return carry

    lax.fori_loop(0, CAP, prepare, 0)
    add_sketch(high_ref, low_ref, table_ref, weight_ref, part_ref, 2 * RHS)


def operator_kernel(
    counts_ref, last_ref, coef_ref, signs_ref, xlo_ref, xhi_ref, ylo_ref, yhi_ref,
    table_ref, weight_ref, pair_high_ref, pair_low_ref, pair_part_ref,
    image_ref, message_ref, gram_ref,
    kap_ref, coupling_ref, high_ref, low_ref, part_ref,
):
    held = held_of(counts_ref)
    lane = iota((8, LANES), 1)
    row = iota((8, LANES), 0)
    kap_ref[...] = jnp.zeros_like(kap_ref)
    for slot in range(CAP):
        kap_ref[slot : slot + 1, :] = coef_ref[slot]

    def kap(j):
        return kap_ref[:, j * LANES : (j + 1) * LANES]

    def low_run(j, here, before, ghost):
        moved = lane_roll(here, PS)
        other = lane_roll(ghost, -PS * ((j // 2) % 8)) if j % 2 == 0 else lane_roll(before, PS)
        return jnp.where(lane < PS, other, moved)

    def high_run(j, here, after, ghost):
        moved = lane_roll(here, -PS)
        other = (
            lane_roll(ghost, LANES - PS - PS * ((j // 2) % 8))
            if j % 2 == 1
            else lane_roll(after, -PS)
        )
        return jnp.where(lane >= LANES - PS, other, moved)

    first = lane % PS == 0
    final = lane % PS == PS - 1
    for j in range(32):
        here = kap(j)
        col = slice((j // 16) * LANES, (j // 16 + 1) * LANES)
        end = slice((j % 2) * LANES, (j % 2 + 1) * LANES)
        if j >= 2:
            below = kap(j - 2)
        else:
            ghost = jnp.broadcast_to(xlo_ref[RHS : RHS + 1, end], (8, LANES))
            below = jnp.where(row == 0, ghost, pltpu.roll(kap(j + 30), 1, 0))
        if j < 30:
            above = kap(j + 2)
        else:
            ghost = jnp.broadcast_to(xhi_ref[RHS : RHS + 1, end], (8, LANES))
            above = jnp.where(row == held - 1, ghost, pltpu.roll(kap(j - 30), 7, 0))
        y_low = low_run(j, here, kap(j - 1) if j % 2 else None, ylo_ref[CAP * RHS :, col])
        y_high = high_run(j, here, None if j % 2 else kap(j + 1), yhi_ref[CAP * RHS :, col])
        z_low = jnp.where(first, 0.0, lane_roll(here, 1))
        z_high = jnp.where(final, 0.0, lane_roll(here, -1))
        weights = [0.5 * (here + near) for near in (below, above, y_low, y_high, z_low, z_high)]
        diagonal = functools.reduce(lambda a, b: a + b, weights)
        weights[4] = jnp.where(first, 0.0, weights[4])
        weights[5] = jnp.where(final, 0.0, weights[5])
        for place, value in enumerate(weights + [diagonal]):
            coupling_ref[place, j, 0:8, :] = value

    gram_ref[...] = jnp.zeros_like(gram_ref)

    def one_slot(slot, carry):
        live = (slot < held).astype(F32)
        flips = (1 - 2 * signs_ref[slot]).astype(F32)
        before_slot = jnp.maximum(slot - 1, 0)
        after_slot = jnp.minimum(slot + 1, CAP - 1)
        for j in range(32):
            lanes = slice(j * LANES, (j + 1) * LANES)
            col = slice((j // 16) * LANES, (j // 16 + 1) * LANES)
            end = slice((j % 2) * LANES, (j % 2 + 1) * LANES)
            coupling = [
                coupling_ref[place, j, pl.ds(slot, 8, stride=0), :]
                for place in range(7)
            ]
            for half in range(2):
                rows = slice(8 * half, 8 * half + 8)

                def cells(s, k):
                    return last_ref[s, 0, rows, k * LANES : (k + 1) * LANES]

                ghost_rows = pl.ds(pl.multiple_of(slot * RHS + 8 * half, 8), 8)
                here = cells(slot, j)
                if j >= 2:
                    below = cells(slot, j - 2)
                else:
                    below = jnp.where(slot == 0, xlo_ref[rows, end], cells(before_slot, j + 30))
                if j < 30:
                    above = cells(slot, j + 2)
                else:
                    above = jnp.where(
                        slot == held - 1, xhi_ref[rows, end], cells(after_slot, j - 30)
                    )
                y_low = low_run(
                    j, here, cells(slot, j - 1) if j % 2 else None, ylo_ref[ghost_rows, col]
                )
                y_high = high_run(
                    j, here, None if j % 2 else cells(slot, j + 1), yhi_ref[ghost_rows, col]
                )
                near = (below, above, y_low, y_high, lane_roll(here, 1), lane_roll(here, -1))
                value = coupling[6] * here
                for weight, neighbour in zip(coupling, near):
                    value = value - weight * neighbour
                image_ref[slot, 0, rows, lanes] = value * live
        for plane in range(PS):
            lanes = slice(plane * FACE, (plane + 1) * FACE)
            high, low = split(image_ref[slot, 0, :, lanes] * flips[:, lanes])
            at = pl.ds(pl.multiple_of((slot * PS + plane) * RHS, 16), RHS)
            high_ref[at, :] = high
            low_ref[at, :] = low
            pair_at = pl.ds(pl.multiple_of((slot * PS + plane) * 32, 32), 32)
            pair_high = pair_high_ref[pair_at, :]
            contract = functools.partial(
                lax.dot_general,
                dimension_numbers=(((1,), (1,)), ((), ())),
                preferred_element_type=F32,
            )
            gram_ref[:, 0:RHS] += (
                contract(pair_high, high)
                + contract(pair_high, low)
                + contract(pair_low_ref[pair_at, :], high)
            )
        return carry

    lax.fori_loop(0, CAP, one_slot, 0)
    add_sketch(high_ref, low_ref, table_ref, weight_ref, part_ref, RHS)
    for col in range(K // LANES):
        lanes = slice(col * LANES, (col + 1) * LANES)
        for tile in range(3):
            if tile == 0:
                top, bottom = pair_part_ref[0:8, lanes], pair_part_ref[24:32, lanes]
            else:
                top = pair_part_ref[8 * tile : 8 * tile + 8, lanes]
                bottom = part_ref[8 * tile - 8 : 8 * tile, lanes]
            rows = slice(8 * tile, 8 * tile + 8)
            message_ref[2 * col, rows, :] = jnp.where(lane < 64, top, lane_roll(bottom, 64))
            message_ref[2 * col + 1, rows, :] = jnp.where(lane < 64, lane_roll(top, 64), bottom)


def sum_kernel(parts_ref, gram_ref, out_ref):
    total = parts_ref[0]
    for source in range(1, GROUP):
        total = total + parts_ref[source]
    out_ref[0:24, :] = total
    out_ref[24:56, :] = gram_ref[...]


def sketch_rows_of(summed_ref):
    return jnp.concatenate([summed_ref[0:24, 0:64], summed_ref[0:24, 64:128]], axis=0)


def gram_kernel(summed_ref, previous_ref, residual_ref, out_ref):
    sketch = sketch_rows_of(summed_ref)
    contract = functools.partial(
        lax.dot_general, precision=highest, preferred_element_type=F32
    )
    first = contract(previous_ref[...], sketch[0:32], dimension_numbers=(((0,), (0,)), ((), ())))
    target = contract(residual_ref[...], sketch[0:16], dimension_numbers=(((0,), (0,)), ((), ())))
    images = jnp.concatenate([first, sketch[32:48]], axis=0)
    whole = jnp.concatenate([images, target], axis=0)
    gram = contract(images, whole, dimension_numbers=(((1,), (1,)), ((), ())))
    piece = jnp.concatenate([gram, summed_ref[24:56, 0:16]], axis=1)
    piece = jnp.concatenate([piece[0:16], piece[16:32]], axis=1)
    for target_index in range(GROUP):
        out_ref[target_index] = piece


def final_kernel(
    counts_ref, parts_ref, summed_ref, old_ref, last_ref, image_ref, new_ref, sketch_ref, solution_ref
):
    held = held_of(counts_ref)
    total = parts_ref[0]
    for source in range(1, GROUP):
        total = total + parts_ref[source]
    matrix = jnp.concatenate([total[:, 0:64], total[:, 64:128]], axis=0)
    projection = matrix[:, 48:64] * (1.0 / NC)
    contract = functools.partial(
        lax.dot_general,
        dimension_numbers=(((0,), (0,)), ((), ())),
        precision=highest,
        preferred_element_type=F32,
    )
    sketch = sketch_rows_of(summed_ref)
    newer = sketch[32:48] - contract(projection, sketch[0:32])
    whole = jnp.concatenate([sketch[0:32], newer], axis=0)
    whole = jnp.concatenate([whole, jnp.zeros_like(whole)], axis=1)
    z_index = lax.axis_index("px") // (N_PX // N_Z)
    moved = pltpu.roll(whole, LANES - z_index * SHARE, 1)
    sketch_ref[...] = moved[:, 0:SHARE]

    def one_slot(slot, carry):
        pair = jnp.concatenate([old_ref[slot, 0], last_ref[slot, 0]], axis=0)
        new = image_ref[slot, 0] - contract(projection, pair)
        new_ref[slot, 0] = jnp.where(slot < held, new, 0.0)
        return carry

    lax.fori_loop(0, CAP, one_slot, 0)

    system = jnp.concatenate([matrix, jnp.zeros((32, 64), F32)], axis=1)
    rows = iota((32, LANES), 0)
    for step in range(32):
        pivot = system[step : step + 1, :]
        scaled = pivot / pivot[:, step : step + 1]
        reduced = system - system[:, step : step + 1] * scaled
        system = jnp.where(rows == step, scaled, reduced)
    solution_ref[...] = system[:, 32:48]


def call(kernel, out_shapes, name, smem=(), scratch=()):
    def run(*args):
        specs = [
            pl.BlockSpec(memory_space=pltpu.SMEM if i in smem else pltpu.VMEM)
            for i in range(len(args))
        ]
        return pl.pallas_call(
            kernel,
            out_shape=[jax.ShapeDtypeStruct(shape, kind) for shape, kind in out_shapes],
            in_specs=specs,
            out_specs=[pl.BlockSpec(memory_space=pltpu.VMEM)] * len(out_shapes),
            scratch_shapes=list(scratch),
            compiler_params=pltpu.CompilerParams(vmem_limit_bytes=56 << 20),
            name=name,
        )(*args)

    return run


def px_pairs(step):
    return [
        (px * N_PY + py, (px + step) * N_PY + py)
        for px in range(N_PX)
        for py in range(N_PY)
        if 0 <= px + step < N_PX
    ]


def py_pairs(step):
    return [
        (px * N_PY + py, px * N_PY + py + step)
        for px in range(N_PX)
        for py in range(N_PY)
        if 0 <= py + step < N_PY
    ]


def z_pairs(step):
    return [
        (px * N_PY + py, (px ^ (step * (N_PX // N_Z))) * N_PY + py)
        for px in range(N_PX)
        for py in range(N_PY)
    ]


def exchange(values):
    groups = [[plane * GROUP + i for i in range(GROUP)] for plane in range(N_Z)]
    return lax.all_to_all(values, AXES, 0, 0, axis_index_groups=groups, tiled=True)


def body(
    counts, coefficient, signs, basis_old, basis_last, residual_factor, previous_coef, sample_rows
):
    x_low, x_high, y_low, y_high = call(
        pack_kernel,
        [((RHS + 8, FACE), F32)] * 2 + [((CAP * RHS + 8, FACE), F32)] * 2,
        "pack",
        smem=(0,),
        scratch=[pltpu.VMEM((8, CELLS), F32)],
    )(counts, basis_last, coefficient)
    ghost_x_low = lax.ppermute(x_high, AXES, px_pairs(1))
    ghost_x_high = lax.ppermute(x_low, AXES, px_pairs(-1))
    ghost_y_low = lax.ppermute(y_high, AXES, py_pairs(1))
    ghost_y_high = lax.ppermute(y_low, AXES, py_pairs(-1))

    rows = sample_rows.reshape(N_Z, GROUP, SHARE).transpose(1, 0, 2).reshape(1, K)
    table, weight, pair_high, pair_low, pair_part = call(
        pair_kernel,
        [
            ((FACE, K), BF16),
            ((CAP * PS, K), F32),
            ((CAP * PS * 32, FACE), BF16),
            ((CAP * PS * 32, FACE), BF16),
            ((32, K), F32),
        ],
        "pair",
        smem=(0,),
    )(counts, rows, basis_old, basis_last, signs)

    image, message, gram = call(
        operator_kernel,
        [
            ((CAP, 1, RHS, CELLS), F32),
            ((GROUP, 24, LANES), F32),
            ((32, LANES), F32),
        ],
        "operator",
        smem=(0,),
        scratch=[
            pltpu.VMEM((8, CELLS), F32),
            pltpu.VMEM((7, 32, 16, LANES), F32),
            pltpu.VMEM((CAP * PS * RHS, FACE), BF16),
            pltpu.VMEM((CAP * PS * RHS, FACE), BF16),
            pltpu.VMEM((RHS, K), F32),
        ],
    )(
        counts, basis_last, coefficient, signs, ghost_x_low, ghost_x_high, ghost_y_low,
        ghost_y_high, table, weight, pair_high, pair_low, pair_part,
    )

    (summed,) = call(sum_kernel, [((56, LANES), F32)], "sum")(exchange(message), gram)
    for step in (1, 2, 4):
        summed = summed + lax.ppermute(summed, AXES, z_pairs(step))
    (pieces,) = call(gram_kernel, [((GROUP, 16, LANES), F32)], "gram")(
        summed, previous_coef, residual_factor
    )
    new_block, sketch, answer = call(
        final_kernel,
        [
            ((CAP, 1, RHS, CELLS), F32),
            ((48, SHARE), F32),
            ((32, 16), F32),
        ],
        "final",
        smem=(0,),
    )(counts, exchange(pieces), summed, basis_old, basis_last, image)
    return (new_block, sketch, answer)


def solution(mesh):
    in_specs = (
        P(),
        P("px", "py", None),
        P("px", "py", None),
        P("px", "py", None, None),
        P("px", "py", None, None),
        P(),
        P(),
        P(),
    )
    out_specs = (P("px", "py", None, None), P(None, ("px", "py")), P())
    return jax.shard_map(body, mesh=mesh, in_specs=in_specs, out_specs=out_specs, check_vma=False)
```

```python
import functools
import math

import jax
import jax.numpy as jnp
from jax import lax
from jax.experimental import pallas as pl
from jax.experimental.pallas import tpu as pltpu
from jax.sharding import PartitionSpec as P

PS = 16
RHS = 16
K = 2048
CAP = 6
CELLS = 4096
NC = 2097152
FACE = PS * PS
LANES = 128
N_PX = 32
N_PY = 8
N_Z = 8
GROUP = 32
SHARE = K // (N_PX * N_PY)
AXES = ("px", "py")

F32 = jnp.float32
BF16 = jnp.bfloat16
highest = lax.Precision.HIGHEST


def iota(shape, dim):
    return lax.broadcasted_iota(jnp.int32, shape, dim)


def sign_of(bits):
    for amount in (8, 4, 2, 1):
        bits = bits ^ (bits >> amount)
    return (1 - 2 * (bits & 1)).astype(F32)


def split(values):
    high = values.astype(BF16)
    return high, (values - high.astype(F32)).astype(BF16)


def lane_roll(tile, shift):
    shift = shift % LANES
    return pltpu.roll(tile, shift, 1) if shift else tile


def held_of(counts_ref):
    return counts_ref[lax.axis_index("px")]


def offset_of(counts_ref):
    index = lax.axis_index("px")
    return lax.fori_loop(
        0, N_PX, lambda i, total: total + jnp.where(i < index, counts_ref[i], 0), jnp.int32(0)
    )


def pack_kernel(counts_ref, last_ref, coef_ref, xlo_ref, xhi_ref, ylo_ref, yhi_ref, kap_ref):
    held = held_of(counts_ref)
    kap_ref[...] = jnp.zeros_like(kap_ref)
    for slot in range(CAP):
        kap_ref[slot : slot + 1, :] = coef_ref[slot]
    xlo_ref[0:RHS, :] = last_ref[0, 0, :, 0:FACE]
    xlo_ref[RHS : RHS + 8, :] = jnp.broadcast_to(kap_ref[0:1, 0:FACE], (8, FACE))
    xhi_ref[0:RHS, :] = last_ref[held - 1, 0, :, CELLS - FACE : CELLS]
    xhi_ref[RHS : RHS + 8, :] = jnp.broadcast_to(
        coef_ref[held - 1, :, CELLS - FACE : CELLS], (8, FACE)
    )
    run = iota((8, LANES), 1) // PS

    def faces(read, row):
        for col in range(2):
            low = jnp.zeros((8, LANES), F32)
            high = jnp.zeros((8, LANES), F32)
            for step in range(8):
                plane = col * 8 + step
                low = jnp.where(run == step, lane_roll(read(2 * plane), PS * step), low)
                high = jnp.where(run == step, lane_roll(read(2 * plane + 1), PS * step + PS), high)
            ylo_ref[pl.ds(row, 8), col * LANES : (col + 1) * LANES] = low
            yhi_ref[pl.ds(row, 8), col * LANES : (col + 1) * LANES] = high

    def one_slot(slot, carry):
        for half in range(2):
            faces(
                lambda j: last_ref[slot, 0, 8 * half : 8 * half + 8, j * LANES : (j + 1) * LANES],
                pl.multiple_of(slot * RHS + 8 * half, 8),
            )
        return carry

    lax.fori_loop(0, CAP, one_slot, 0)
    faces(lambda j: kap_ref[:, j * LANES : (j + 1) * LANES], CAP * RHS)


def add_sketch(high_ref, low_ref, table_ref, weight_ref, out_ref, rows):
    out_ref[...] = jnp.zeros_like(out_ref)

    def one_slot(slot, carry):
        at = pl.ds(pl.multiple_of(slot * PS * rows, 16), PS * rows)
        high = high_ref[at, :]
        low = low_ref[at, :]
        for block in range(K // 256):
            lanes = slice(block * 256, (block + 1) * 256)
            table = table_ref[:, lanes]
            mixed = jnp.dot(high, table, preferred_element_type=F32) + jnp.dot(
                low, table, preferred_element_type=F32
            )
            weight = weight_ref[pl.ds(pl.multiple_of(slot * PS, 16), PS), lanes]
            total = out_ref[:, lanes]
            for plane in range(PS):
                total = total + weight[plane : plane + 1] * mixed[plane * rows : (plane + 1) * rows]
            out_ref[:, lanes] = total
        return carry

    lax.fori_loop(0, CAP, one_slot, 0)


def pair_kernel(
    counts_ref, rows_ref, old_ref, last_ref, signs_ref,
    table_ref, weight_ref, high_ref, low_ref, part_ref,
):
    held = held_of(counts_ref)
    offset = offset_of(counts_ref)
    rows = rows_ref[...]
    index = iota((16, K), 0)
    inner = sign_of(index & (rows & 15))
    outer = sign_of(index & ((rows >> 4) & 15))
    for step in range(16):
        table_ref[16 * step : 16 * step + 16, :] = (inner * outer[step : step + 1]).astype(BF16)
    plane_sign = sign_of(index & ((rows >> 8) & 15))
    slot_ids = iota((8, K), 0)
    patch = (offset + slot_ids) * N_PY + lax.axis_index("py")
    slot_sign = sign_of(patch & (rows >> 12)) * jnp.where(
        slot_ids < held, 1.0 / math.sqrt(NC), 0.0
    )
    for slot in range(CAP):
        weight_ref[slot * PS : (slot + 1) * PS, :] = plane_sign * slot_sign[slot : slot + 1]

    def prepare(slot, carry):
        flips = (1 - 2 * signs_ref[slot]).astype(F32)
        for place, ref in ((0, old_ref), (1, last_ref)):
            high, low = split(ref[slot, 0] * flips)
            for plane in range(PS):
                at = pl.ds(pl.multiple_of((slot * PS + plane) * 32 + 16 * place, 16), 16)
                high_ref[at, :] = high[:, plane * FACE : (plane + 1) * FACE]
                low_ref[at, :] = low[:, plane * FACE : (plane + 1) * FACE]
        return carry

    lax.fori_loop(0, CAP, prepare, 0)
    add_sketch(high_ref, low_ref, table_ref, weight_ref, part_ref, 2 * RHS)


def operator_kernel(
    counts_ref, last_ref, coef_ref, signs_ref, xlo_ref, xhi_ref, ylo_ref, yhi_ref,
    table_ref, weight_ref, pair_high_ref, pair_low_ref, pair_part_ref,
    image_ref, message_ref, gram_ref,
    kap_ref, coupling_ref, high_ref, low_ref, part_ref,
):
    held = held_of(counts_ref)
    lane = iota((8, LANES), 1)
    row = iota((8, LANES), 0)
    kap_ref[...] = jnp.zeros_like(kap_ref)
    for slot in range(CAP):
        kap_ref[slot : slot + 1, :] = coef_ref[slot]

    def kap(j):
        return kap_ref[:, j * LANES : (j + 1) * LANES]

    def low_run(j, here, before, ghost):
        moved = lane_roll(here, PS)
        other = lane_roll(ghost, -PS * ((j // 2) % 8)) if j % 2 == 0 else lane_roll(before, PS)
        return jnp.where(lane < PS, other, moved)

    def high_run(j, here, after, ghost):
        moved = lane_roll(here, -PS)
        other = (
            lane_roll(ghost, LANES - PS - PS * ((j // 2) % 8))
            if j % 2 == 1
            else lane_roll(after, -PS)
        )
        return jnp.where(lane >= LANES - PS, other, moved)

    first = lane % PS == 0
    final = lane % PS == PS - 1
    for j in range(32):
        here = kap(j)
        col = slice((j // 16) * LANES, (j // 16 + 1) * LANES)
        end = slice((j % 2) * LANES, (j % 2 + 1) * LANES)
        if j >= 2:
            below = kap(j - 2)
        else:
            ghost = jnp.broadcast_to(xlo_ref[RHS : RHS + 1, end], (8, LANES))
            below = jnp.where(row == 0, ghost, pltpu.roll(kap(j + 30), 1, 0))
        if j < 30:
            above = kap(j + 2)
        else:
            ghost = jnp.broadcast_to(xhi_ref[RHS : RHS + 1, end], (8, LANES))
            above = jnp.where(row == held - 1, ghost, pltpu.roll(kap(j - 30), 7, 0))
        y_low = low_run(j, here, kap(j - 1) if j % 2 else None, ylo_ref[CAP * RHS :, col])
        y_high = high_run(j, here, None if j % 2 else kap(j + 1), yhi_ref[CAP * RHS :, col])
        z_low = jnp.where(first, 0.0, lane_roll(here, 1))
        z_high = jnp.where(final, 0.0, lane_roll(here, -1))
        weights = [0.5 * (here + near) for near in (below, above, y_low, y_high, z_low, z_high)]
        diagonal = functools.reduce(lambda a, b: a + b, weights)
        weights[4] = jnp.where(first, 0.0, weights[4])
        weights[5] = jnp.where(final, 0.0, weights[5])
        for place, value in enumerate(weights + [diagonal]):
            coupling_ref[place, j, 0:8, :] = value

    gram_ref[...] = jnp.zeros_like(gram_ref)

    def one_slot(slot, carry):
        live = (slot < held).astype(F32)
        flips = (1 - 2 * signs_ref[slot]).astype(F32)
        before_slot = jnp.maximum(slot - 1, 0)
        after_slot = jnp.minimum(slot + 1, CAP - 1)
        for j in range(32):
            lanes = slice(j * LANES, (j + 1) * LANES)
            col = slice((j // 16) * LANES, (j // 16 + 1) * LANES)
            end = slice((j % 2) * LANES, (j % 2 + 1) * LANES)
            coupling = [
                coupling_ref[place, j, pl.ds(slot, 8, stride=0), :]
                for place in range(7)
            ]
            for half in range(2):
                rows = slice(8 * half, 8 * half + 8)

                def cells(s, k):
                    return last_ref[s, 0, rows, k * LANES : (k + 1) * LANES]

                ghost_rows = pl.ds(pl.multiple_of(slot * RHS + 8 * half, 8), 8)
                here = cells(slot, j)
                if j >= 2:
                    below = cells(slot, j - 2)
                else:
                    below = jnp.where(slot == 0, xlo_ref[rows, end], cells(before_slot, j + 30))
                if j < 30:
                    above = cells(slot, j + 2)
                else:
                    above = jnp.where(
                        slot == held - 1, xhi_ref[rows, end], cells(after_slot, j - 30)
                    )
                y_low = low_run(
                    j, here, cells(slot, j - 1) if j % 2 else None, ylo_ref[ghost_rows, col]
                )
                y_high = high_run(
                    j, here, None if j % 2 else cells(slot, j + 1), yhi_ref[ghost_rows, col]
                )
                near = (below, above, y_low, y_high, lane_roll(here, 1), lane_roll(here, -1))
                value = coupling[6] * here
                for weight, neighbour in zip(coupling, near):
                    value = value - weight * neighbour
                image_ref[slot, 0, rows, lanes] = value * live
        for plane in range(PS):
            lanes = slice(plane * FACE, (plane + 1) * FACE)
            high, low = split(image_ref[slot, 0, :, lanes] * flips[:, lanes])
            at = pl.ds(pl.multiple_of((slot * PS + plane) * RHS, 16), RHS)
            high_ref[at, :] = high
            low_ref[at, :] = low
            pair_at = pl.ds(pl.multiple_of((slot * PS + plane) * 32, 32), 32)
            pair_high = pair_high_ref[pair_at, :]
            contract = functools.partial(
                lax.dot_general,
                dimension_numbers=(((1,), (1,)), ((), ())),
                preferred_element_type=F32,
            )
            gram_ref[:, 0:RHS] += (
                contract(pair_high, high)
                + contract(pair_high, low)
                + contract(pair_low_ref[pair_at, :], high)
            )
        return carry

    lax.fori_loop(0, CAP, one_slot, 0)
    add_sketch(high_ref, low_ref, table_ref, weight_ref, part_ref, RHS)
    for col in range(K // LANES):
        lanes = slice(col * LANES, (col + 1) * LANES)
        for tile in range(3):
            if tile == 0:
                top, bottom = pair_part_ref[0:8, lanes], pair_part_ref[24:32, lanes]
            else:
                top = pair_part_ref[8 * tile : 8 * tile + 8, lanes]
                bottom = part_ref[8 * tile - 8 : 8 * tile, lanes]
            rows = slice(8 * tile, 8 * tile + 8)
            message_ref[2 * col, rows, :] = jnp.where(lane < 64, top, lane_roll(bottom, 64))
            message_ref[2 * col + 1, rows, :] = jnp.where(lane < 64, lane_roll(top, 64), bottom)


def sum_kernel(parts_ref, gram_ref, out_ref):
    total = parts_ref[0]
    for source in range(1, GROUP):
        total = total + parts_ref[source]
    gram = gram_ref[0:8, :]
    for tile in range(1, 4):
        gram = gram + lane_roll(gram_ref[8 * tile : 8 * tile + 8, :], RHS * tile)
    for target in range(N_Z):
        out_ref[target, 0:24, :] = total
        out_ref[target, 24:32, :] = gram


def gram_kernel(parts_ref, previous_ref, residual_ref, out_ref, sketch_ref):
    summed = parts_ref[0]
    for source in range(1, N_Z):
        summed = summed + parts_ref[source]
    sketch = jnp.concatenate([summed[0:24, 0:64], summed[0:24, 64:128]], axis=0)
    sketch_ref[...] = sketch
    contract = functools.partial(
        lax.dot_general, precision=highest, preferred_element_type=F32
    )
    first = contract(previous_ref[...], sketch[0:32], dimension_numbers=(((1,), (0,)), ((), ())))
    target = contract(residual_ref[...], sketch[0:16], dimension_numbers=(((0,), (0,)), ((), ())))
    images = jnp.concatenate([first, sketch[32:48]], axis=0)
    whole = jnp.concatenate([images, target], axis=0)
    gram = contract(images, whole, dimension_numbers=(((1,), (1,)), ((), ())))
    product = jnp.concatenate(
        [lane_roll(summed[24:32], -RHS * tile)[:, 0:RHS] for tile in range(4)], axis=0
    )
    piece = jnp.concatenate([gram, product], axis=1)
    piece = jnp.concatenate([piece[0:16], piece[16:32]], axis=1)
    for target_index in range(GROUP):
        out_ref[target_index] = piece


def final_kernel(
    counts_ref, parts_ref, rows_ref, old_ref, last_ref, image_ref, new_ref, sketch_ref, solution_ref
):
    held = held_of(counts_ref)
    total = parts_ref[0]
    for source in range(1, GROUP):
        total = total + parts_ref[source]
    matrix = jnp.concatenate([total[:, 0:64], total[:, 64:128]], axis=0)
    projection = matrix[:, 48:64] * (1.0 / NC)
    contract = functools.partial(
        lax.dot_general,
        dimension_numbers=(((0,), (0,)), ((), ())),
        precision=highest,
        preferred_element_type=F32,
    )
    sketch = rows_ref[...]
    newer = sketch[32:48] - contract(projection, sketch[0:32])
    whole = jnp.concatenate([sketch[0:32], newer], axis=0)
    whole = jnp.concatenate([whole, jnp.zeros_like(whole)], axis=1)
    z_index = lax.axis_index("px") // (N_PX // N_Z)
    moved = pltpu.roll(whole, LANES - z_index * SHARE, 1)
    sketch_ref[...] = moved.T[0:SHARE, :]

    def one_slot(slot, carry):
        pair = jnp.concatenate([old_ref[slot, 0], last_ref[slot, 0]], axis=0)
        new = image_ref[slot, 0] - contract(projection, pair)
        new_ref[slot, 0] = jnp.where(slot < held, new, 0.0)
        return carry

    lax.fori_loop(0, CAP, one_slot, 0)

    system = jnp.concatenate([matrix, jnp.zeros((32, 64), F32)], axis=1)
    rows = iota((32, LANES), 0)
    for step in range(32):
        pivot = system[step : step + 1, :]
        scaled = pivot / pivot[:, step : step + 1]
        reduced = system - system[:, step : step + 1] * scaled
        system = jnp.where(rows == step, scaled, reduced)
    solution_ref[...] = system.T[32:48, :]


def call(kernel, out_shapes, name, smem=(), scratch=(), near_in=(), near_out=()):
    def run(*args):
        args = [
            pltpu.with_memory_space_constraint(value, pltpu.VMEM) if i in near_in else value
            for i, value in enumerate(args)
        ]
        specs = [
            pl.BlockSpec(memory_space=pltpu.SMEM if i in smem else pltpu.VMEM)
            for i in range(len(args))
        ]
        return pl.pallas_call(
            kernel,
            out_shape=[
                (pltpu.VMEM if i in near_out else jax.ShapeDtypeStruct)(shape, kind)
                for i, (shape, kind) in enumerate(out_shapes)
            ],
            in_specs=specs,
            out_specs=[pl.BlockSpec(memory_space=pltpu.VMEM)] * len(out_shapes),
            scratch_shapes=list(scratch),
            compiler_params=pltpu.CompilerParams(vmem_limit_bytes=24 << 20),
            name=name,
        )(*args)

    return run


def px_pairs(step):
    return [
        (px * N_PY + py, (px + step) * N_PY + py)
        for px in range(N_PX)
        for py in range(N_PY)
        if 0 <= px + step < N_PX
    ]


def py_pairs(step):
    return [
        (px * N_PY + py, px * N_PY + py + step)
        for px in range(N_PX)
        for py in range(N_PY)
        if 0 <= py + step < N_PY
    ]


def exchange(values, along_z=False):
    groups = [[plane * GROUP + i for i in range(GROUP)] for plane in range(N_Z)]
    if along_z:
        groups = [list(members) for members in zip(*groups)]
    return lax.all_to_all(values, AXES, 0, 0, axis_index_groups=groups, tiled=True)


def body(
    counts, coefficient, signs, basis_old, basis_last, residual_factor, previous_coef, sample_rows
):
    x_low, x_high, y_low, y_high = call(
        pack_kernel,
        [((RHS + 8, FACE), F32)] * 2 + [((CAP * RHS + 8, FACE), F32)] * 2,
        "pack",
        smem=(0,),
        scratch=[pltpu.VMEM((8, CELLS), F32)],
    )(counts, basis_last, coefficient)
    ghost_x_low = lax.ppermute(x_high, AXES, px_pairs(1))
    ghost_x_high = lax.ppermute(x_low, AXES, px_pairs(-1))
    ghost_y_low = lax.ppermute(y_high, AXES, py_pairs(1))
    ghost_y_high = lax.ppermute(y_low, AXES, py_pairs(-1))

    rows = sample_rows.reshape(N_Z, GROUP, SHARE).transpose(1, 0, 2).reshape(1, K)
    table, weight, pair_high, pair_low, pair_part = call(
        pair_kernel,
        [
            ((FACE, K), BF16),
            ((CAP * PS, K), F32),
            ((CAP * PS * 32, FACE), BF16),
            ((CAP * PS * 32, FACE), BF16),
            ((32, K), F32),
        ],
        "pair",
        smem=(0,),
        near_in=(2, 3),
        near_out=range(5),
    )(counts, rows, basis_old, basis_last, signs)

    image, message, gram = call(
        operator_kernel,
        [
            ((CAP, 1, RHS, CELLS), F32),
            ((GROUP, 24, LANES), F32),
            ((32, LANES), F32),
        ],
        "operator",
        smem=(0,),
        near_in=(1, 4, 5, 6, 7, 8, 9, 10, 11, 12),
        near_out=(0, 2),
        scratch=[
            pltpu.VMEM((8, CELLS), F32),
            pltpu.VMEM((7, 32, 16, LANES), F32),
            pltpu.VMEM((CAP * PS * RHS, FACE), BF16),
            pltpu.VMEM((CAP * PS * RHS, FACE), BF16),
            pltpu.VMEM((RHS, K), F32),
        ],
    )(
        counts, basis_last, coefficient, signs, ghost_x_low, ghost_x_high, ghost_y_low,
        ghost_y_high, table, weight, pair_high, pair_low, pair_part,
    )

    (summed,) = call(sum_kernel, [((N_Z, 32, LANES), F32)], "sum", near_in=(0, 1))(exchange(message), gram)
    pieces, chunk = call(
        gram_kernel, [((GROUP, 16, LANES), F32), ((48, 64), F32)], "gram", near_in=(0,), near_out=(1,)
    )(exchange(summed, along_z=True), previous_coef.T, residual_factor)
    new_block, sketch, answer = call(
        final_kernel,
        [
            ((CAP, 1, RHS, CELLS), F32),
            ((SHARE, 48), F32),
            ((16, 32), F32),
        ],
        "final",
        smem=(0,),
        near_in=(1, 2, 3, 4, 5),
    )(counts, exchange(pieces), chunk, basis_old, basis_last, image)
    return (new_block, sketch.T, answer.T)


def solution(mesh):
    in_specs = (
        P(),
        P("px", "py", None),
        P("px", "py", None),
        P("px", "py", None, None),
        P("px", "py", None, None),
        P(),
        P(),
        P(),
    )
    out_specs = (P("px", "py", None, None), P(None, ("px", "py")), P())
    return jax.shard_map(body, mesh=mesh, in_specs=in_specs, out_specs=out_specs, check_vma=False)
```

```python
import functools
import math

import jax
import jax.numpy as jnp
from jax import lax
from jax.experimental import pallas as pl
from jax.experimental.pallas import tpu as pltpu
from jax.sharding import PartitionSpec as P

PS = 16
RHS = 16
K = 2048
CAP = 6
CELLS = 4096
NC = 2097152
FACE = PS * PS
LANES = 128
N_PX = 32
N_PY = 8
N_Z = 8
GROUP = 32
SHARE = K // (N_PX * N_PY)
AXES = ("px", "py")

F32 = jnp.float32
BF16 = jnp.bfloat16
highest = lax.Precision.HIGHEST


def iota(shape, dim):
    return lax.broadcasted_iota(jnp.int32, shape, dim)


def sign_of(bits):
    for amount in (8, 4, 2, 1):
        bits = bits ^ (bits >> amount)
    return (1 - 2 * (bits & 1)).astype(F32)


def split(values):
    high = values.astype(BF16)
    return high, (values - high.astype(F32)).astype(BF16)


def lane_roll(tile, shift):
    shift = shift % LANES
    return pltpu.roll(tile, shift, 1) if shift else tile


def held_of(counts_ref):
    return counts_ref[lax.axis_index("px")]


def offset_of(counts_ref):
    index = lax.axis_index("px")
    return lax.fori_loop(
        0, N_PX, lambda i, total: total + jnp.where(i < index, counts_ref[i], 0), jnp.int32(0)
    )


def pack_kernel(
    counts_hbm, last_hbm, coef_hbm, xeven_ref, xodd_ref, yeven_ref, yodd_ref,
    counts_ref, last_ref, coef_ref, kap_ref, sems,
):
    copies = [
        pltpu.make_async_copy(source, target, sems.at[i])
        for i, (source, target) in enumerate(
            ((counts_hbm, counts_ref), (coef_hbm, coef_ref), (last_hbm, last_ref))
        )
    ]
    for copy in copies:
        copy.start()
    for copy in copies:
        copy.wait()
    held = held_of(counts_ref)
    x_even = lax.axis_index("px") % 2 == 0
    y_even = lax.axis_index("py") % 2 == 0
    kap_ref[...] = jnp.zeros_like(kap_ref)
    for slot in range(CAP):
        kap_ref[slot : slot + 1, :] = coef_ref[slot]
    low = last_ref[0, 0, :, 0:FACE]
    high = last_ref[held - 1, 0, :, CELLS - FACE : CELLS]
    xeven_ref[0:RHS, :] = jnp.where(x_even, high, low)
    xodd_ref[0:RHS, :] = jnp.where(x_even, low, high)
    low = jnp.broadcast_to(kap_ref[0:1, 0:FACE], (8, FACE))
    high = jnp.broadcast_to(coef_ref[held - 1, :, CELLS - FACE : CELLS], (8, FACE))
    xeven_ref[RHS : RHS + 8, :] = jnp.where(x_even, high, low)
    xodd_ref[RHS : RHS + 8, :] = jnp.where(x_even, low, high)
    run = iota((8, LANES), 1) // PS

    def faces(read, row):
        for col in range(2):
            low = jnp.zeros((8, LANES), F32)
            high = jnp.zeros((8, LANES), F32)
            for step in range(8):
                plane = col * 8 + step
                low = jnp.where(run == step, lane_roll(read(2 * plane), PS * step), low)
                high = jnp.where(run == step, lane_roll(read(2 * plane + 1), PS * step + PS), high)
            lanes = slice(col * LANES, (col + 1) * LANES)
            yeven_ref[pl.ds(row, 8), lanes] = jnp.where(y_even, high, low)
            yodd_ref[pl.ds(row, 8), lanes] = jnp.where(y_even, low, high)

    def one_slot(slot, carry):
        for half in range(2):
            faces(
                lambda j: last_ref[slot, 0, 8 * half : 8 * half + 8, j * LANES : (j + 1) * LANES],
                pl.multiple_of(slot * RHS + 8 * half, 8),
            )
        return carry

    lax.fori_loop(0, CAP, one_slot, 0)
    faces(lambda j: kap_ref[:, j * LANES : (j + 1) * LANES], CAP * RHS)


def add_sketch(high_ref, low_ref, table_ref, weight_ref, out_ref, rows):
    out_ref[...] = jnp.zeros_like(out_ref)

    def one_slot(slot, carry):
        at = pl.ds(pl.multiple_of(slot * PS * rows, 16), PS * rows)
        high = high_ref[at, :]
        low = low_ref[at, :]
        for block in range(K // 256):
            lanes = slice(block * 256, (block + 1) * 256)
            table = table_ref[:, lanes]
            mixed = jnp.dot(high, table, preferred_element_type=F32) + jnp.dot(
                low, table, preferred_element_type=F32
            )
            weight = weight_ref[pl.ds(pl.multiple_of(slot * PS, 16), PS), lanes]
            total = out_ref[:, lanes]
            for plane in range(PS):
                total = total + weight[plane : plane + 1] * mixed[plane * rows : (plane + 1) * rows]
            out_ref[:, lanes] = total
        return carry

    lax.fori_loop(0, CAP, one_slot, 0)


def permuted(rows_ref):
    group = iota((8, LANES), 1) // SHARE
    tiles = []
    for col in range(16):
        tile = jnp.zeros((8, LANES), jnp.int32)
        for z in range(N_Z):
            here = jnp.broadcast_to(rows_ref[2 * z + col // 8 : 2 * z + col // 8 + 1, :], (8, LANES))
            base = 16 * (col % 8)
            tile = jnp.where(group == z, lane_roll(here, SHARE * z - base), tile)
            tile = jnp.where(group == N_Z + z, lane_roll(here, 64 + SHARE * z - base - 8), tile)
        tiles.append(tile[0:1])
    return jnp.concatenate(tiles, axis=1)


def pair_kernel(
    counts_ref, rows_ref, old_hbm, last_hbm, signs_ref,
    table_ref, weight_ref, high_ref, low_ref, part_ref, old_ref, last_ref, sems,
):
    copies = [
        pltpu.make_async_copy(source, target, sems.at[i])
        for i, (source, target) in enumerate(((old_hbm, old_ref), (last_hbm, last_ref)))
    ]
    for copy in copies:
        copy.start()
    held = held_of(counts_ref)
    offset = offset_of(counts_ref)
    rows = permuted(rows_ref)
    index = iota((16, K), 0)
    inner = sign_of(index & (rows & 15))
    outer = sign_of(index & ((rows >> 4) & 15))
    for step in range(16):
        table_ref[16 * step : 16 * step + 16, :] = (inner * outer[step : step + 1]).astype(BF16)
    plane_sign = sign_of(index & ((rows >> 8) & 15))
    slot_ids = iota((8, K), 0)
    patch = (offset + slot_ids) * N_PY + lax.axis_index("py")
    slot_sign = sign_of(patch & (rows >> 12)) * jnp.where(
        slot_ids < held, 1.0 / math.sqrt(NC), 0.0
    )
    for slot in range(CAP):
        weight_ref[slot * PS : (slot + 1) * PS, :] = plane_sign * slot_sign[slot : slot + 1]

    for copy in copies:
        copy.wait()

    def prepare(slot, carry):
        flips = (1 - 2 * signs_ref[slot]).astype(F32)
        for place, ref in ((0, old_ref), (1, last_ref)):
            high, low = split(ref[slot, 0] * flips)
            for plane in range(PS):
                at = pl.ds(pl.multiple_of((slot * PS + plane) * 32 + 16 * place, 16), 16)
                high_ref[at, :] = high[:, plane * FACE : (plane + 1) * FACE]
                low_ref[at, :] = low[:, plane * FACE : (plane + 1) * FACE]
        return carry

    lax.fori_loop(0, CAP, prepare, 0)
    add_sketch(high_ref, low_ref, table_ref, weight_ref, part_ref, 2 * RHS)


def operator_kernel(
    counts_ref, last_ref, coef_ref, signs_ref, xeven_ref, xodd_ref, yeven_ref, yodd_ref,
    table_ref, weight_ref, pair_high_ref, pair_low_ref, pair_part_ref,
    image_ref, message_ref, gram_ref,
    kap_ref, coupling_ref, high_ref, low_ref, part_ref, xlo_ref, xhi_ref, ylo_ref, yhi_ref,
):
    held = held_of(counts_ref)
    x_even = lax.axis_index("px") % 2 == 0
    y_even = lax.axis_index("py") % 2 == 0
    xlo_ref[...] = jnp.where(x_even, xodd_ref[...], xeven_ref[...])
    xhi_ref[...] = jnp.where(x_even, xeven_ref[...], xodd_ref[...])
    ylo_ref[...] = jnp.where(y_even, yodd_ref[...], yeven_ref[...])
    yhi_ref[...] = jnp.where(y_even, yeven_ref[...], yodd_ref[...])
    lane = iota((8, LANES), 1)
    row = iota((8, LANES), 0)
    kap_ref[...] = jnp.zeros_like(kap_ref)
    for slot in range(CAP):
        kap_ref[slot : slot + 1, :] = coef_ref[slot]

    def kap(j):
        return kap_ref[:, j * LANES : (j + 1) * LANES]

    def low_run(j, here, before, ghost):
        moved = lane_roll(here, PS)
        other = lane_roll(ghost, -PS * ((j // 2) % 8)) if j % 2 == 0 else lane_roll(before, PS)
        return jnp.where(lane < PS, other, moved)

    def high_run(j, here, after, ghost):
        moved = lane_roll(here, -PS)
        other = (
            lane_roll(ghost, LANES - PS - PS * ((j // 2) % 8))
            if j % 2 == 1
            else lane_roll(after, -PS)
        )
        return jnp.where(lane >= LANES - PS, other, moved)

    first = lane % PS == 0
    final = lane % PS == PS - 1
    for j in range(32):
        here = kap(j)
        col = slice((j // 16) * LANES, (j // 16 + 1) * LANES)
        end = slice((j % 2) * LANES, (j % 2 + 1) * LANES)
        if j >= 2:
            below = kap(j - 2)
        else:
            ghost = jnp.broadcast_to(xlo_ref[RHS : RHS + 1, end], (8, LANES))
            below = jnp.where(row == 0, ghost, pltpu.roll(kap(j + 30), 1, 0))
        if j < 30:
            above = kap(j + 2)
        else:
            ghost = jnp.broadcast_to(xhi_ref[RHS : RHS + 1, end], (8, LANES))
            above = jnp.where(row == held - 1, ghost, pltpu.roll(kap(j - 30), 7, 0))
        y_low = low_run(j, here, kap(j - 1) if j % 2 else None, ylo_ref[CAP * RHS :, col])
        y_high = high_run(j, here, None if j % 2 else kap(j + 1), yhi_ref[CAP * RHS :, col])
        z_low = jnp.where(first, 0.0, lane_roll(here, 1))
        z_high = jnp.where(final, 0.0, lane_roll(here, -1))
        weights = [0.5 * (here + near) for near in (below, above, y_low, y_high, z_low, z_high)]
        diagonal = functools.reduce(lambda a, b: a + b, weights)
        weights[4] = jnp.where(first, 0.0, weights[4])
        weights[5] = jnp.where(final, 0.0, weights[5])
        for place, value in enumerate(weights + [diagonal]):
            coupling_ref[place, j, 0:8, :] = value

    gram_ref[...] = jnp.zeros_like(gram_ref)

    def one_slot(slot, carry):
        live = (slot < held).astype(F32)
        flips = (1 - 2 * signs_ref[slot]).astype(F32)
        before_slot = jnp.maximum(slot - 1, 0)
        after_slot = jnp.minimum(slot + 1, CAP - 1)
        for j in range(32):
            lanes = slice(j * LANES, (j + 1) * LANES)
            col = slice((j // 16) * LANES, (j // 16 + 1) * LANES)
            end = slice((j % 2) * LANES, (j % 2 + 1) * LANES)
            coupling = [
                coupling_ref[place, j, pl.ds(slot, 8, stride=0), :]
                for place in range(7)
            ]
            for half in range(2):
                rows = slice(8 * half, 8 * half + 8)

                def cells(s, k):
                    return last_ref[s, 0, rows, k * LANES : (k + 1) * LANES]

                ghost_rows = pl.ds(pl.multiple_of(slot * RHS + 8 * half, 8), 8)
                here = cells(slot, j)
                if j >= 2:
                    below = cells(slot, j - 2)
                else:
                    below = jnp.where(slot == 0, xlo_ref[rows, end], cells(before_slot, j + 30))
                if j < 30:
                    above = cells(slot, j + 2)
                else:
                    above = jnp.where(
                        slot == held - 1, xhi_ref[rows, end], cells(after_slot, j - 30)
                    )
                y_low = low_run(
                    j, here, cells(slot, j - 1) if j % 2 else None, ylo_ref[ghost_rows, col]
                )
                y_high = high_run(
                    j, here, None if j % 2 else cells(slot, j + 1), yhi_ref[ghost_rows, col]
                )
                near = (below, above, y_low, y_high, lane_roll(here, 1), lane_roll(here, -1))
                value = coupling[6] * here
                for weight, neighbour in zip(coupling, near):
                    value = value - weight * neighbour
                image_ref[slot, 0, rows, lanes] = value * live
        for plane in range(PS):
            lanes = slice(plane * FACE, (plane + 1) * FACE)
            high, low = split(image_ref[slot, 0, :, lanes] * flips[:, lanes])
            at = pl.ds(pl.multiple_of((slot * PS + plane) * RHS, 16), RHS)
            high_ref[at, :] = high
            low_ref[at, :] = low
            pair_at = pl.ds(pl.multiple_of((slot * PS + plane) * 32, 32), 32)
            pair_high = pair_high_ref[pair_at, :]
            contract = functools.partial(
                lax.dot_general,
                dimension_numbers=(((1,), (1,)), ((), ())),
                preferred_element_type=F32,
            )
            gram_ref[:, 0:RHS] += (
                contract(pair_high, high)
                + contract(pair_high, low)
                + contract(pair_low_ref[pair_at, :], high)
            )
        return carry

    lax.fori_loop(0, CAP, one_slot, 0)
    add_sketch(high_ref, low_ref, table_ref, weight_ref, part_ref, RHS)
    for col in range(K // LANES):
        lanes = slice(col * LANES, (col + 1) * LANES)
        for tile in range(3):
            if tile == 0:
                top, bottom = pair_part_ref[0:8, lanes], pair_part_ref[24:32, lanes]
            else:
                top = pair_part_ref[8 * tile : 8 * tile + 8, lanes]
                bottom = part_ref[8 * tile - 8 : 8 * tile, lanes]
            rows = slice(8 * tile, 8 * tile + 8)
            message_ref[2 * col, rows, :] = jnp.where(lane < 64, top, lane_roll(bottom, 64))
            message_ref[2 * col + 1, rows, :] = jnp.where(lane < 64, lane_roll(top, 64), bottom)


def sum_kernel(parts_ref, gram_ref, out_ref):
    total = parts_ref[0]
    for source in range(1, GROUP):
        total = total + parts_ref[source]
    gram = gram_ref[0:8, :]
    for tile in range(1, 4):
        gram = gram + lane_roll(gram_ref[8 * tile : 8 * tile + 8, :], RHS * tile)
    for target in range(N_Z):
        out_ref[target, 0:24, :] = total
        out_ref[target, 24:32, :] = gram


def gram_kernel(parts_ref, previous_ref, residual_ref, out_ref, sketch_ref):
    summed = parts_ref[0]
    for source in range(1, N_Z):
        summed = summed + parts_ref[source]
    sketch = jnp.concatenate([summed[0:24, 0:64], summed[0:24, 64:128]], axis=0)
    sketch_ref[...] = sketch
    contract = functools.partial(
        lax.dot_general, precision=highest, preferred_element_type=F32
    )
    first = contract(previous_ref[...], sketch[0:32], dimension_numbers=(((1,), (0,)), ((), ())))
    target = contract(residual_ref[...], sketch[0:16], dimension_numbers=(((0,), (0,)), ((), ())))
    images = jnp.concatenate([first, sketch[32:48]], axis=0)
    whole = jnp.concatenate([images, target], axis=0)
    gram = contract(images, whole, dimension_numbers=(((1,), (1,)), ((), ())))
    product = jnp.concatenate(
        [lane_roll(summed[24:32], -RHS * tile)[:, 0:RHS] for tile in range(4)], axis=0
    )
    piece = jnp.concatenate([gram, product], axis=1)
    piece = jnp.concatenate([piece[0:16], piece[16:32]], axis=1)
    for target_index in range(GROUP):
        out_ref[target_index] = piece


def final_kernel(
    counts_ref, parts_ref, rows_ref, signs_ref, high_ref, low_ref, image_ref,
    new_hbm, sketch_ref, solution_ref, new_ref, sems,
):
    held = held_of(counts_ref)
    total = parts_ref[0]
    for source in range(1, GROUP):
        total = total + parts_ref[source]
    matrix = jnp.concatenate([total[:, 0:64], total[:, 64:128]], axis=0)
    projection = (matrix[:, 48:64] * (1.0 / NC)).T
    system = jnp.concatenate([matrix, jnp.zeros((32, 64), F32)], axis=1)
    row_ids = iota((32, LANES), 0)
    large, small = split(projection)
    both = jnp.concatenate([large, small], axis=0)
    copies = []
    step = 0
    for slot in range(CAP):
        flips = (1 - 2 * signs_ref[slot]).astype(F32)
        for plane in range(PS):
            lanes = slice(plane * FACE, (plane + 1) * FACE)
            at = slice((slot * PS + plane) * 32, (slot * PS + plane + 1) * 32)
            mixed = jnp.dot(both, high_ref[at, :], preferred_element_type=F32)
            mixed_low = jnp.dot(large, low_ref[at, :], preferred_element_type=F32)
            change = (mixed[0:RHS] + mixed[RHS:] + mixed_low) * flips[:, lanes]
            new = image_ref[slot, 0, :, lanes] - change
            new_ref[slot, 0, :, lanes] = jnp.where(slot < held, new, 0.0)
            if plane % 3 == 0 and step < 32:
                pivot = system[step : step + 1, :]
                scaled = pivot / pivot[:, step : step + 1]
                reduced = system - system[:, step : step + 1] * scaled
                system = jnp.where(row_ids == step, scaled, reduced)
                step += 1
        copies.append(pltpu.make_async_copy(new_ref.at[slot], new_hbm.at[slot], sems.at[slot]))
        copies[-1].start()
    solution_ref[...] = system.T[32:48, :]
    sketch = rows_ref[...]
    newer = sketch[32:48] - jnp.dot(
        projection, sketch[0:32], precision=highest, preferred_element_type=F32
    )
    whole = jnp.concatenate([sketch[0:32], newer], axis=0)
    whole = jnp.concatenate([whole, jnp.zeros_like(whole)], axis=1)
    z_index = lax.axis_index("px") // (N_PX // N_Z)
    moved = pltpu.roll(whole, LANES - z_index * SHARE, 1)
    sketch_ref[...] = moved.T[0:SHARE, :]
    for copy in copies:
        copy.wait()


def call(kernel, out_shapes, name, smem=(), scratch=(), near_in=(), near_out=(), far_in=(), far_out=()):
    def run(*args):
        args = [
            pltpu.with_memory_space_constraint(value, pltpu.VMEM if i in near_in else pltpu.HBM)
            if i in near_in or i in far_in
            else value
            for i, value in enumerate(args)
        ]
        specs = [
            pl.BlockSpec(
                memory_space=pltpu.SMEM if i in smem else pltpu.HBM if i in far_in else pltpu.VMEM
            )
            for i in range(len(args))
        ]
        return pl.pallas_call(
            kernel,
            out_shape=[
                (pltpu.VMEM if i in near_out else jax.ShapeDtypeStruct)(shape, kind)
                for i, (shape, kind) in enumerate(out_shapes)
            ],
            in_specs=specs,
            out_specs=[
                pl.BlockSpec(memory_space=pltpu.HBM if i in far_out else pltpu.VMEM)
                for i in range(len(out_shapes))
            ],
            scratch_shapes=list(scratch),
            compiler_params=pltpu.CompilerParams(vmem_limit_bytes=24 << 20),
            name=name,
        )(*args)

    return run


def partner(index, first, size):
    other = index + 1 if index % 2 == first else index - 1
    return other if 0 <= other < size else None


def px_pairs(first):
    return [
        (px * N_PY + py, partner(px, first, N_PX) * N_PY + py)
        for px in range(N_PX)
        for py in range(N_PY)
        if partner(px, first, N_PX) is not None
    ]


def py_pairs(first):
    return [
        (px * N_PY + py, px * N_PY + partner(py, first, N_PY))
        for px in range(N_PX)
        for py in range(N_PY)
        if partner(py, first, N_PY) is not None
    ]


def exchange(values, along_z=False):
    groups = [[plane * GROUP + i for i in range(GROUP)] for plane in range(N_Z)]
    if along_z:
        groups = [list(members) for members in zip(*groups)]
    return lax.all_to_all(values, AXES, 0, 0, axis_index_groups=groups, tiled=True)


def body(
    counts, coefficient, signs, basis_old, basis_last, residual_factor, previous_coef, sample_rows
):
    faces = call(
        pack_kernel,
        [((RHS + 8, FACE), F32)] * 2 + [((CAP * RHS + 8, FACE), F32)] * 2,
        "pack",
        far_in=(0, 1, 2),
        scratch=[
            pltpu.SMEM((N_PX,), jnp.int32),
            pltpu.VMEM((CAP, 1, RHS, CELLS), F32),
            pltpu.VMEM((CAP, 1, CELLS), F32),
            pltpu.VMEM((8, CELLS), F32),
            pltpu.SemaphoreType.DMA((3,)),
        ],
    )(counts, basis_last, coefficient)
    ghosts = [
        lax.ppermute(face, AXES, pairs)
        for face, pairs in zip(faces, (px_pairs(0), px_pairs(1), py_pairs(0), py_pairs(1)))
    ]

    rows = sample_rows.reshape(K // LANES, LANES)
    table, weight, pair_high, pair_low, pair_part = call(
        pair_kernel,
        [
            ((FACE, K), BF16),
            ((CAP * PS, K), F32),
            ((CAP * PS * 32, FACE), BF16),
            ((CAP * PS * 32, FACE), BF16),
            ((32, K), F32),
        ],
        "pair",
        smem=(0,),
        far_in=(2, 3),
        near_out=range(5),
        scratch=[pltpu.VMEM((CAP, 1, RHS, CELLS), F32)] * 2 + [pltpu.SemaphoreType.DMA((2,))],
    )(counts, rows, basis_old, basis_last, signs)

    image, message, gram = call(
        operator_kernel,
        [
            ((CAP, 1, RHS, CELLS), F32),
            ((GROUP, 24, LANES), F32),
            ((32, LANES), F32),
        ],
        "operator",
        smem=(0,),
        near_in=(1, 4, 5, 6, 7, 8, 9, 10, 11, 12),
        near_out=(0, 2),
        scratch=[
            pltpu.VMEM((8, CELLS), F32),
            pltpu.VMEM((7, 32, 16, LANES), F32),
            pltpu.VMEM((CAP * PS * RHS, FACE), BF16),
            pltpu.VMEM((CAP * PS * RHS, FACE), BF16),
            pltpu.VMEM((RHS, K), F32),
        ]
        + [pltpu.VMEM((RHS + 8, FACE), F32)] * 2
        + [pltpu.VMEM((CAP * RHS + 8, FACE), F32)] * 2,
    )(
        counts, basis_last, coefficient, signs, *ghosts, table, weight, pair_high, pair_low, pair_part,
    )

    (summed,) = call(sum_kernel, [((N_Z, 32, LANES), F32)], "sum", near_in=(0, 1))(exchange(message), gram)
    pieces, chunk = call(
        gram_kernel, [((GROUP, 16, LANES), F32), ((48, 64), F32)], "gram", near_in=(0,), near_out=(1,)
    )(exchange(summed, along_z=True), previous_coef.T, residual_factor)
    new_block, sketch, answer = call(
        final_kernel,
        [
            ((CAP, 1, RHS, CELLS), F32),
            ((SHARE, 48), F32),
            ((16, 32), F32),
        ],
        "final",
        smem=(0,),
        near_in=(1, 2, 3, 4, 5, 6),
        far_out=(0,),
        scratch=[pltpu.VMEM((CAP, 1, RHS, CELLS), F32), pltpu.SemaphoreType.DMA((CAP,))],
    )(counts, exchange(pieces), chunk, signs, pair_high, pair_low, image)
    return (new_block, sketch.T, answer.T)


def solution(mesh):
    in_specs = (
        P(),
        P("px", "py", None),
        P("px", "py", None),
        P("px", "py", None, None),
        P("px", "py", None, None),
        P(),
        P(),
        P(),
    )
    out_specs = (P("px", "py", None, None), P(None, ("px", "py")), P())
    return jax.shard_map(body, mesh=mesh, in_specs=in_specs, out_specs=out_specs, check_vma=False)
```

```python
import functools
import math

import jax
import jax.numpy as jnp
from jax import lax
from jax.experimental import pallas as pl
from jax.experimental.pallas import tpu as pltpu
from jax.sharding import PartitionSpec as P

PS = 16
RHS = 16
K = 2048
CAP = 6
CELLS = 4096
NC = 2097152
FACE = PS * PS
LANES = 128
N_PX = 32
N_PY = 8
N_Z = 8
GROUP = 32
EARLY = 4
SHARE = K // (N_PX * N_PY)
AXES = ("px", "py")

F32 = jnp.float32
BF16 = jnp.bfloat16
highest = lax.Precision.HIGHEST


def iota(shape, dim):
    return lax.broadcasted_iota(jnp.int32, shape, dim)


def sign_of(bits):
    for amount in (8, 4, 2, 1):
        bits = bits ^ (bits >> amount)
    return (1 - 2 * (bits & 1)).astype(F32)


def split(values):
    high = values.astype(BF16)
    return high, (values - high.astype(F32)).astype(BF16)


def lane_roll(tile, shift):
    shift = shift % LANES
    return pltpu.roll(tile, shift, 1) if shift else tile


def held_of(counts_ref):
    return counts_ref[lax.axis_index("px")]


def offset_of(counts_ref):
    index = lax.axis_index("px")
    return lax.fori_loop(
        0, N_PX, lambda i, total: total + jnp.where(i < index, counts_ref[i], 0), jnp.int32(0)
    )


def pack_kernel(
    counts_hbm, last_hbm, coef_hbm, xeven_ref, xodd_ref, yeven_ref, yodd_ref,
    counts_ref, last_ref, coef_ref, kap_ref, sems,
):
    copies = [
        pltpu.make_async_copy(source, target, sems.at[i])
        for i, (source, target) in enumerate(
            ((counts_hbm, counts_ref), (coef_hbm, coef_ref), (last_hbm, last_ref))
        )
    ]
    for copy in copies:
        copy.start()
    for copy in copies:
        copy.wait()
    held = held_of(counts_ref)
    x_even = lax.axis_index("px") % 2 == 0
    y_even = lax.axis_index("py") % 2 == 0
    kap_ref[...] = jnp.zeros_like(kap_ref)
    for slot in range(CAP):
        kap_ref[slot : slot + 1, :] = coef_ref[slot]
    low = last_ref[0, 0, :, 0:FACE]
    high = last_ref[held - 1, 0, :, CELLS - FACE : CELLS]
    xeven_ref[0:RHS, :] = jnp.where(x_even, high, low)
    xodd_ref[0:RHS, :] = jnp.where(x_even, low, high)
    low = jnp.broadcast_to(kap_ref[0:1, 0:FACE], (8, FACE))
    high = jnp.broadcast_to(coef_ref[held - 1, :, CELLS - FACE : CELLS], (8, FACE))
    xeven_ref[RHS : RHS + 8, :] = jnp.where(x_even, high, low)
    xodd_ref[RHS : RHS + 8, :] = jnp.where(x_even, low, high)
    run = iota((8, LANES), 1) // PS

    def faces(read, row):
        for col in range(2):
            low = jnp.zeros((8, LANES), F32)
            high = jnp.zeros((8, LANES), F32)
            for step in range(8):
                plane = col * 8 + step
                low = jnp.where(run == step, lane_roll(read(2 * plane), PS * step), low)
                high = jnp.where(run == step, lane_roll(read(2 * plane + 1), PS * step + PS), high)
            lanes = slice(col * LANES, (col + 1) * LANES)
            yeven_ref[pl.ds(row, 8), lanes] = jnp.where(y_even, high, low)
            yodd_ref[pl.ds(row, 8), lanes] = jnp.where(y_even, low, high)

    def one_slot(slot, carry):
        for half in range(2):
            faces(
                lambda j: last_ref[slot, 0, 8 * half : 8 * half + 8, j * LANES : (j + 1) * LANES],
                pl.multiple_of(slot * RHS + 8 * half, 8),
            )
        return carry

    lax.fori_loop(0, CAP, one_slot, 0)
    faces(lambda j: kap_ref[:, j * LANES : (j + 1) * LANES], CAP * RHS)


def add_block(slot, block, high_ref, low_ref, table_ref, weight_ref, out_ref, rows):
    at = slice(slot * PS * rows, (slot + 1) * PS * rows)
    lanes = slice(block * 256, (block + 1) * 256)
    table = table_ref[:, lanes]
    mixed = jnp.dot(high_ref[at, :], table, preferred_element_type=F32) + jnp.dot(
        low_ref[at, :], table, preferred_element_type=F32
    )
    weight = weight_ref[slot * PS : (slot + 1) * PS, lanes]
    total = out_ref[:, lanes]
    for plane in range(PS):
        total = total + weight[plane : plane + 1] * mixed[plane * rows : (plane + 1) * rows]
    out_ref[:, lanes] = total


def permuted(rows_ref):
    group = iota((8, LANES), 1) // SHARE
    tiles = []
    for col in range(16):
        tile = jnp.zeros((8, LANES), jnp.int32)
        for z in range(N_Z):
            here = jnp.broadcast_to(rows_ref[2 * z + col // 8 : 2 * z + col // 8 + 1, :], (8, LANES))
            base = 16 * (col % 8)
            tile = jnp.where(group == z, lane_roll(here, SHARE * z - base), tile)
            tile = jnp.where(group == N_Z + z, lane_roll(here, 64 + SHARE * z - base - 8), tile)
        tiles.append(tile[0:1])
    return jnp.concatenate(tiles, axis=1)


def pair_kernel(
    counts_ref, rows_ref, old_hbm, last_hbm, signs_ref,
    table_ref, weight_ref, high_ref, low_ref, part_ref, old_ref, last_ref, sems,
):
    copies = [
        pltpu.make_async_copy(source, target, sems.at[i])
        for i, (source, target) in enumerate(((old_hbm, old_ref), (last_hbm, last_ref)))
    ]
    for copy in copies:
        copy.start()
    held = held_of(counts_ref)
    offset = offset_of(counts_ref)
    rows = permuted(rows_ref)
    index = iota((16, K), 0)
    inner = sign_of(index & (rows & 15))
    outer = sign_of(index & ((rows >> 4) & 15))
    for step in range(16):
        table_ref[16 * step : 16 * step + 16, :] = (inner * outer[step : step + 1]).astype(BF16)
    plane_sign = sign_of(index & ((rows >> 8) & 15))
    slot_ids = iota((8, K), 0)
    patch = (offset + slot_ids) * N_PY + lax.axis_index("py")
    slot_sign = sign_of(patch & (rows >> 12)) * jnp.where(
        slot_ids < held, 1.0 / math.sqrt(NC), 0.0
    )
    for slot in range(CAP):
        weight_ref[slot * PS : (slot + 1) * PS, :] = plane_sign * slot_sign[slot : slot + 1]

    for copy in copies:
        copy.wait()

    def prepare(slot, place, ref, planes):
        flips = (1 - 2 * signs_ref[slot]).astype(F32)
        for plane in planes:
            lanes = slice(plane * FACE, (plane + 1) * FACE)
            high, low = split(ref[slot, 0, :, lanes] * flips[:, lanes])
            row = (slot * PS + plane) * 32 + RHS * place
            high_ref[row : row + RHS, :] = high
            low_ref[row : row + RHS, :] = low

    part_ref[...] = jnp.zeros_like(part_ref)
    for slot in range(CAP + 1):
        for block in range(8):
            if slot < CAP:
                for place, ref in ((0, old_ref), (1, last_ref)):
                    prepare(slot, place, ref, (2 * block, 2 * block + 1))
            if 0 < slot <= EARLY:
                add_block(
                    slot - 1, block, high_ref, low_ref, table_ref, weight_ref, part_ref, 2 * RHS
                )


def operator_kernel(
    counts_ref, last_ref, coef_ref, signs_ref, xeven_ref, xodd_ref, yeven_ref, yodd_ref,
    table_ref, weight_ref, pair_high_ref, pair_low_ref, pair_part_ref,
    image_ref, message_ref, gram_ref,
    kap_ref, coupling_ref, high_ref, low_ref, part_ref, sum_ref, xlo_ref, xhi_ref, ylo_ref, yhi_ref,
):
    held = held_of(counts_ref)
    x_even = lax.axis_index("px") % 2 == 0
    y_even = lax.axis_index("py") % 2 == 0
    xlo_ref[...] = jnp.where(x_even, xodd_ref[...], xeven_ref[...])
    xhi_ref[...] = jnp.where(x_even, xeven_ref[...], xodd_ref[...])
    ylo_ref[...] = jnp.where(y_even, yodd_ref[...], yeven_ref[...])
    yhi_ref[...] = jnp.where(y_even, yeven_ref[...], yodd_ref[...])
    lane = iota((8, LANES), 1)
    row = iota((8, LANES), 0)
    kap_ref[...] = jnp.zeros_like(kap_ref)
    for slot in range(CAP):
        kap_ref[slot : slot + 1, :] = coef_ref[slot]

    def kap(j):
        return kap_ref[:, j * LANES : (j + 1) * LANES]

    def low_run(j, here, before, ghost):
        moved = lane_roll(here, PS)
        other = lane_roll(ghost, -PS * ((j // 2) % 8)) if j % 2 == 0 else lane_roll(before, PS)
        return jnp.where(lane < PS, other, moved)

    def high_run(j, here, after, ghost):
        moved = lane_roll(here, -PS)
        other = (
            lane_roll(ghost, LANES - PS - PS * ((j // 2) % 8))
            if j % 2 == 1
            else lane_roll(after, -PS)
        )
        return jnp.where(lane >= LANES - PS, other, moved)

    first = lane % PS == 0
    final = lane % PS == PS - 1
    for j in range(32):
        here = kap(j)
        col = slice((j // 16) * LANES, (j // 16 + 1) * LANES)
        end = slice((j % 2) * LANES, (j % 2 + 1) * LANES)
        if j >= 2:
            below = kap(j - 2)
        else:
            ghost = jnp.broadcast_to(xlo_ref[RHS : RHS + 1, end], (8, LANES))
            below = jnp.where(row == 0, ghost, pltpu.roll(kap(j + 30), 1, 0))
        if j < 30:
            above = kap(j + 2)
        else:
            ghost = jnp.broadcast_to(xhi_ref[RHS : RHS + 1, end], (8, LANES))
            above = jnp.where(row == held - 1, ghost, pltpu.roll(kap(j - 30), 7, 0))
        y_low = low_run(j, here, kap(j - 1) if j % 2 else None, ylo_ref[CAP * RHS :, col])
        y_high = high_run(j, here, None if j % 2 else kap(j + 1), yhi_ref[CAP * RHS :, col])
        z_low = jnp.where(first, 0.0, lane_roll(here, 1))
        z_high = jnp.where(final, 0.0, lane_roll(here, -1))
        weights = [0.5 * (here + near) for near in (below, above, y_low, y_high, z_low, z_high)]
        diagonal = functools.reduce(lambda a, b: a + b, weights)
        weights[4] = jnp.where(first, 0.0, weights[4])
        weights[5] = jnp.where(final, 0.0, weights[5])
        for place, value in enumerate(weights + [diagonal]):
            coupling_ref[place, j, 0:8, :] = value

    gram_ref[...] = jnp.zeros_like(gram_ref)
    part_ref[...] = jnp.zeros_like(part_ref)
    sum_ref[...] = pair_part_ref[...]
    contract = functools.partial(
        lax.dot_general,
        dimension_numbers=(((1,), (1,)), ((), ())),
        preferred_element_type=F32,
    )

    def stencil(slot, j):
        live = (slot < held).astype(F32)
        lanes = slice(j * LANES, (j + 1) * LANES)
        col = slice((j // 16) * LANES, (j // 16 + 1) * LANES)
        end = slice((j % 2) * LANES, (j % 2 + 1) * LANES)
        coupling = [
            jnp.broadcast_to(coupling_ref[place, j, slot : slot + 1, :], (8, LANES))
            for place in range(7)
        ]
        for half in range(2):
            rows = slice(8 * half, 8 * half + 8)

            def cells(s, k):
                return last_ref[s, 0, rows, k * LANES : (k + 1) * LANES]

            ghost_rows = slice(slot * RHS + 8 * half, slot * RHS + 8 * half + 8)
            here = cells(slot, j)
            if j >= 2:
                below = cells(slot, j - 2)
            else:
                below = cells(slot - 1, j + 30) if slot else xlo_ref[rows, end]
            if j < 30:
                above = cells(slot, j + 2)
            else:
                above = xhi_ref[rows, end]
                if slot < CAP - 1:
                    above = jnp.where(slot == held - 1, above, cells(slot + 1, j - 30))
            y_low = low_run(
                j, here, cells(slot, j - 1) if j % 2 else None, ylo_ref[ghost_rows, col]
            )
            y_high = high_run(
                j, here, None if j % 2 else cells(slot, j + 1), yhi_ref[ghost_rows, col]
            )
            near = (below, above, y_low, y_high, lane_roll(here, 1), lane_roll(here, -1))
            value = coupling[6] * here
            for weight, neighbour in zip(coupling, near):
                value = value - weight * neighbour
            image_ref[slot, 0, rows, lanes] = value * live

    def finish(slot, plane, flips):
        lanes = slice(plane * FACE, (plane + 1) * FACE)
        high, low = split(image_ref[slot, 0, :, lanes] * flips[:, lanes])
        at = slice((slot * PS + plane) * RHS, (slot * PS + plane + 1) * RHS)
        high_ref[at, :] = high
        low_ref[at, :] = low
        pair_at = slice((slot * PS + plane) * 32, (slot * PS + plane + 1) * 32)
        pair_high = pair_high_ref[pair_at, :]
        return (
            contract(pair_high, high)
            + contract(pair_high, low)
            + contract(pair_low_ref[pair_at, :], high)
        )

    for slot in range(CAP + 1):
        if slot < CAP:
            flips = (1 - 2 * signs_ref[slot]).astype(F32)
            gram = gram_ref[:, 0:RHS]
        for block in range(8):
            if slot < CAP:
                for j in range(4 * block, 4 * block + 4):
                    stencil(slot, j)
                for plane in (2 * block, 2 * block + 1):
                    gram = gram + finish(slot, plane, flips)
            if slot:
                add_block(
                    slot - 1, block, high_ref, low_ref, table_ref, weight_ref, part_ref, RHS
                )
            if slot < CAP - EARLY:
                add_block(
                    EARLY + slot, block, pair_high_ref, pair_low_ref, table_ref, weight_ref,
                    sum_ref, 2 * RHS,
                )
        if slot < CAP:
            gram_ref[:, 0:RHS] = gram
    for col in range(K // LANES):
        lanes = slice(col * LANES, (col + 1) * LANES)
        for tile in range(3):
            if tile == 0:
                top, bottom = sum_ref[0:8, lanes], sum_ref[24:32, lanes]
            else:
                top = sum_ref[8 * tile : 8 * tile + 8, lanes]
                bottom = part_ref[8 * tile - 8 : 8 * tile, lanes]
            rows = slice(8 * tile, 8 * tile + 8)
            message_ref[2 * col, rows, :] = jnp.where(lane < 64, top, lane_roll(bottom, 64))
            message_ref[2 * col + 1, rows, :] = jnp.where(lane < 64, lane_roll(top, 64), bottom)


def sum_kernel(parts_ref, gram_ref, out_ref):
    total = parts_ref[0]
    for source in range(1, GROUP):
        total = total + parts_ref[source]
    gram = gram_ref[0:8, :]
    for tile in range(1, 4):
        gram = gram + lane_roll(gram_ref[8 * tile : 8 * tile + 8, :], RHS * tile)
    for target in range(N_Z):
        out_ref[target, 0:24, :] = total
        out_ref[target, 24:32, :] = gram


def gram_kernel(parts_ref, previous_ref, residual_ref, out_ref, sketch_ref):
    summed = parts_ref[0]
    for source in range(1, N_Z):
        summed = summed + parts_ref[source]
    sketch = jnp.concatenate([summed[0:24, 0:64], summed[0:24, 64:128]], axis=0)
    sketch_ref[...] = sketch
    contract = functools.partial(
        lax.dot_general, precision=highest, preferred_element_type=F32
    )
    first = contract(previous_ref[...], sketch[0:32], dimension_numbers=(((1,), (0,)), ((), ())))
    target = contract(residual_ref[...], sketch[0:16], dimension_numbers=(((0,), (0,)), ((), ())))
    images = jnp.concatenate([first, sketch[32:48]], axis=0)
    whole = jnp.concatenate([images, target], axis=0)
    gram = contract(images, whole, dimension_numbers=(((1,), (1,)), ((), ())))
    product = jnp.concatenate(
        [lane_roll(summed[24:32], -RHS * tile)[:, 0:RHS] for tile in range(4)], axis=0
    )
    piece = jnp.concatenate([gram, product], axis=1)
    piece = jnp.concatenate([piece[0:16], piece[16:32]], axis=1)
    for target_index in range(GROUP):
        out_ref[target_index] = piece


def final_kernel(
    counts_ref, parts_ref, rows_ref, signs_ref, high_ref, low_ref, image_ref,
    new_hbm, sketch_ref, solution_ref, new_ref, sems,
):
    held = held_of(counts_ref)
    total = parts_ref[0]
    for source in range(1, GROUP):
        total = total + parts_ref[source]
    matrix = jnp.concatenate([total[:, 0:64], total[:, 64:128]], axis=0)
    projection = (matrix[:, 48:64] * (1.0 / NC)).T
    system = jnp.concatenate([matrix, jnp.zeros((32, 64), F32)], axis=1)
    row_ids = iota((32, LANES), 0)
    large, small = split(projection)
    both = jnp.concatenate([large, small], axis=0)
    copies = []
    step = 0
    for slot in range(CAP):
        flips = (1 - 2 * signs_ref[slot]).astype(F32)
        for plane in range(PS):
            lanes = slice(plane * FACE, (plane + 1) * FACE)
            at = slice((slot * PS + plane) * 32, (slot * PS + plane + 1) * 32)
            mixed = jnp.dot(both, high_ref[at, :], preferred_element_type=F32)
            mixed_low = jnp.dot(large, low_ref[at, :], preferred_element_type=F32)
            change = (mixed[0:RHS] + mixed[RHS:] + mixed_low) * flips[:, lanes]
            new = image_ref[slot, 0, :, lanes] - change
            new_ref[slot, 0, :, lanes] = jnp.where(slot < held, new, 0.0)
            if plane % 3 == 0 and step < 32:
                pivot = system[step : step + 1, :]
                scaled = pivot / pivot[:, step : step + 1]
                reduced = system - system[:, step : step + 1] * scaled
                system = jnp.where(row_ids == step, scaled, reduced)
                step += 1
        copies.append(pltpu.make_async_copy(new_ref.at[slot], new_hbm.at[slot], sems.at[slot]))
        copies[-1].start()
    solution_ref[...] = system.T[32:48, :]
    sketch = rows_ref[...]
    newer = sketch[32:48] - jnp.dot(
        projection, sketch[0:32], precision=highest, preferred_element_type=F32
    )
    whole = jnp.concatenate([sketch[0:32], newer], axis=0)
    whole = jnp.concatenate([whole, jnp.zeros_like(whole)], axis=1)
    z_index = lax.axis_index("px") // (N_PX // N_Z)
    moved = pltpu.roll(whole, LANES - z_index * SHARE, 1)
    sketch_ref[...] = moved.T[0:SHARE, :]
    for copy in copies:
        copy.wait()


def call(kernel, out_shapes, name, smem=(), scratch=(), near_in=(), near_out=(), far_in=(), far_out=()):
    def run(*args):
        args = [
            pltpu.with_memory_space_constraint(value, pltpu.VMEM if i in near_in else pltpu.HBM)
            if i in near_in or i in far_in
            else value
            for i, value in enumerate(args)
        ]
        specs = [
            pl.BlockSpec(
                memory_space=pltpu.SMEM if i in smem else pltpu.HBM if i in far_in else pltpu.VMEM
            )
            for i in range(len(args))
        ]
        return pl.pallas_call(
            kernel,
            out_shape=[
                (pltpu.VMEM if i in near_out else jax.ShapeDtypeStruct)(shape, kind)
                for i, (shape, kind) in enumerate(out_shapes)
            ],
            in_specs=specs,
            out_specs=[
                pl.BlockSpec(memory_space=pltpu.HBM if i in far_out else pltpu.VMEM)
                for i in range(len(out_shapes))
            ],
            scratch_shapes=list(scratch),
            compiler_params=pltpu.CompilerParams(vmem_limit_bytes=24 << 20),
            name=name,
        )(*args)

    return run


def partner(index, first, size):
    other = index + 1 if index % 2 == first else index - 1
    return other if 0 <= other < size else None


def px_pairs(first):
    return [
        (px * N_PY + py, partner(px, first, N_PX) * N_PY + py)
        for px in range(N_PX)
        for py in range(N_PY)
        if partner(px, first, N_PX) is not None
    ]


def py_pairs(first):
    return [
        (px * N_PY + py, px * N_PY + partner(py, first, N_PY))
        for px in range(N_PX)
        for py in range(N_PY)
        if partner(py, first, N_PY) is not None
    ]


def exchange(values, along_z=False):
    groups = [[plane * GROUP + i for i in range(GROUP)] for plane in range(N_Z)]
    if along_z:
        groups = [list(members) for members in zip(*groups)]
    return lax.all_to_all(values, AXES, 0, 0, axis_index_groups=groups, tiled=True)


def body(
    counts, coefficient, signs, basis_old, basis_last, residual_factor, previous_coef, sample_rows
):
    faces = call(
        pack_kernel,
        [((RHS + 8, FACE), F32)] * 2 + [((CAP * RHS + 8, FACE), F32)] * 2,
        "pack",
        far_in=(0, 1, 2),
        scratch=[
            pltpu.SMEM((N_PX,), jnp.int32),
            pltpu.VMEM((CAP, 1, RHS, CELLS), F32),
            pltpu.VMEM((CAP, 1, CELLS), F32),
            pltpu.VMEM((8, CELLS), F32),
            pltpu.SemaphoreType.DMA((3,)),
        ],
    )(counts, basis_last, coefficient)
    ghosts = [
        lax.ppermute(face, AXES, pairs)
        for face, pairs in zip(faces, (px_pairs(0), px_pairs(1), py_pairs(0), py_pairs(1)))
    ]

    rows = sample_rows.reshape(K // LANES, LANES)
    table, weight, pair_high, pair_low, pair_part = call(
        pair_kernel,
        [
            ((FACE, K), BF16),
            ((CAP * PS, K), F32),
            ((CAP * PS * 32, FACE), BF16),
            ((CAP * PS * 32, FACE), BF16),
            ((32, K), F32),
        ],
        "pair",
        smem=(0,),
        far_in=(2, 3),
        near_out=range(5),
        scratch=[pltpu.VMEM((CAP, 1, RHS, CELLS), F32)] * 2 + [pltpu.SemaphoreType.DMA((2,))],
    )(counts, rows, basis_old, basis_last, signs)

    image, message, gram = call(
        operator_kernel,
        [
            ((CAP, 1, RHS, CELLS), F32),
            ((GROUP, 24, LANES), F32),
            ((32, LANES), F32),
        ],
        "operator",
        smem=(0,),
        near_in=(1, 4, 5, 6, 7, 8, 9, 10, 11, 12),
        near_out=(0, 2),
        scratch=[
            pltpu.VMEM((8, CELLS), F32),
            pltpu.VMEM((7, 32, 8, LANES), F32),
            pltpu.VMEM((CAP * PS * RHS, FACE), BF16),
            pltpu.VMEM((CAP * PS * RHS, FACE), BF16),
            pltpu.VMEM((RHS, K), F32),
            pltpu.VMEM((2 * RHS, K), F32),
        ]
        + [pltpu.VMEM((RHS + 8, FACE), F32)] * 2
        + [pltpu.VMEM((CAP * RHS + 8, FACE), F32)] * 2,
    )(
        counts, basis_last, coefficient, signs, *ghosts, table, weight, pair_high, pair_low, pair_part,
    )

    (summed,) = call(sum_kernel, [((N_Z, 32, LANES), F32)], "sum", near_in=(0, 1))(exchange(message), gram)
    pieces, chunk = call(
        gram_kernel, [((GROUP, 16, LANES), F32), ((48, 64), F32)], "gram", near_in=(0,), near_out=(1,)
    )(exchange(summed, along_z=True), previous_coef.T, residual_factor)
    new_block, sketch, answer = call(
        final_kernel,
        [
            ((CAP, 1, RHS, CELLS), F32),
            ((SHARE, 48), F32),
            ((16, 32), F32),
        ],
        "final",
        smem=(0,),
        near_in=(1, 2, 3, 4, 5, 6),
        far_out=(0,),
        scratch=[pltpu.VMEM((CAP, 1, RHS, CELLS), F32), pltpu.SemaphoreType.DMA((CAP,))],
    )(counts, exchange(pieces), chunk, signs, pair_high, pair_low, image)
    return (new_block, sketch.T, answer.T)


def solution(mesh):
    in_specs = (
        P(),
        P("px", "py", None),
        P("px", "py", None),
        P("px", "py", None, None),
        P("px", "py", None, None),
        P(),
        P(),
        P(),
    )
    out_specs = (P("px", "py", None, None), P(None, ("px", "py")), P())
    return jax.shard_map(body, mesh=mesh, in_specs=in_specs, out_specs=out_specs, check_vma=False)
```

```python
import functools
import math

import jax
import jax.numpy as jnp
from jax import lax
from jax.experimental import pallas as pl
from jax.experimental.pallas import tpu as pltpu
from jax.sharding import PartitionSpec as P

PS = 16
RHS = 16
K = 2048
CAP = 6
CELLS = 4096
NC = 2097152
FACE = PS * PS
LANES = 128
N_PX = 32
N_PY = 8
N_Z = 8
GROUP = 32
EARLY = 4
SHARE = K // (N_PX * N_PY)
AXES = ("px", "py")

F32 = jnp.float32
BF16 = jnp.bfloat16
highest = lax.Precision.HIGHEST


def iota(shape, dim):
    return lax.broadcasted_iota(jnp.int32, shape, dim)


def sign_of(bits):
    for amount in (8, 4, 2, 1):
        bits = bits ^ (bits >> amount)
    return (1 - 2 * (bits & 1)).astype(F32)


def split(values):
    high = values.astype(BF16)
    return high, (values - high.astype(F32)).astype(BF16)


def lane_roll(tile, shift):
    shift = shift % LANES
    return pltpu.roll(tile, shift, 1) if shift else tile


def held_of(counts_ref):
    return counts_ref[lax.axis_index("px")]


def offset_of(counts_ref):
    index = lax.axis_index("px")
    return lax.fori_loop(
        0, N_PX, lambda i, total: total + jnp.where(i < index, counts_ref[i], 0), jnp.int32(0)
    )


def permuted(rows_ref):
    group = iota((8, LANES), 1) // SHARE
    tiles = []
    for col in range(16):
        tile = jnp.zeros((8, LANES), jnp.int32)
        for z in range(N_Z):
            here = jnp.broadcast_to(rows_ref[2 * z + col // 8 : 2 * z + col // 8 + 1, :], (8, LANES))
            base = 16 * (col % 8)
            tile = jnp.where(group == z, lane_roll(here, SHARE * z - base), tile)
            tile = jnp.where(group == N_Z + z, lane_roll(here, 64 + SHARE * z - base - 8), tile)
        tiles.append(tile[0:1])
    return jnp.concatenate(tiles, axis=1)


def make_tables(counts_ref, held, rows_ref, table_ref, weight_ref):
    offset = offset_of(counts_ref)
    rows = permuted(rows_ref)
    index = iota((16, K), 0)
    inner = sign_of(index & (rows & 15))
    outer = sign_of(index & ((rows >> 4) & 15))
    for step in range(16):
        table_ref[16 * step : 16 * step + 16, :] = (inner * outer[step : step + 1]).astype(BF16)
    plane_sign = sign_of(index & ((rows >> 8) & 15))
    slot_ids = iota((8, K), 0)
    patch = (offset + slot_ids) * N_PY + lax.axis_index("py")
    slot_sign = sign_of(patch & (rows >> 12)) * jnp.where(
        slot_ids < held, 1.0 / math.sqrt(NC), 0.0
    )
    for slot in range(CAP):
        weight_ref[slot * PS : (slot + 1) * PS, :] = plane_sign * slot_sign[slot : slot + 1]


def pack_kernel(
    counts_hbm, rows_hbm, coef_hbm, last_hbm, old_hbm,
    xeven_ref, xodd_ref, yeven_ref, yodd_ref, table_ref, weight_ref, last_ref, old_ref,
    counts_ref, rows_ref, coef_ref, kap_ref, sems,
):
    copies = [
        pltpu.make_async_copy(source, target, sems.at[i])
        for i, (source, target) in enumerate(
            (
                (counts_hbm, counts_ref), (rows_hbm, rows_ref), (coef_hbm, coef_ref),
                (last_hbm, last_ref), (old_hbm, old_ref),
            )
        )
    ]
    for copy in copies:
        copy.start()
    copies[0].wait()
    copies[1].wait()
    held = held_of(counts_ref)
    make_tables(counts_ref, held, rows_ref, table_ref, weight_ref)
    copies[2].wait()
    copies[3].wait()
    x_even = lax.axis_index("px") % 2 == 0
    y_even = lax.axis_index("py") % 2 == 0
    kap_ref[...] = jnp.zeros_like(kap_ref)
    for slot in range(CAP):
        kap_ref[slot : slot + 1, :] = coef_ref[slot]
    low = last_ref[0, 0, :, 0:FACE]
    high = last_ref[held - 1, 0, :, CELLS - FACE : CELLS]
    xeven_ref[0:RHS, :] = jnp.where(x_even, high, low)
    xodd_ref[0:RHS, :] = jnp.where(x_even, low, high)
    low = jnp.broadcast_to(kap_ref[0:1, 0:FACE], (8, FACE))
    high = jnp.broadcast_to(coef_ref[held - 1, :, CELLS - FACE : CELLS], (8, FACE))
    xeven_ref[RHS : RHS + 8, :] = jnp.where(x_even, high, low)
    xodd_ref[RHS : RHS + 8, :] = jnp.where(x_even, low, high)
    run = iota((8, LANES), 1) // PS

    def faces(read, row):
        for col in range(2):
            low = jnp.zeros((8, LANES), F32)
            high = jnp.zeros((8, LANES), F32)
            for step in range(8):
                plane = col * 8 + step
                low = jnp.where(run == step, lane_roll(read(2 * plane), PS * step), low)
                high = jnp.where(run == step, lane_roll(read(2 * plane + 1), PS * step + PS), high)
            lanes = slice(col * LANES, (col + 1) * LANES)
            yeven_ref[pl.ds(row, 8), lanes] = jnp.where(y_even, high, low)
            yodd_ref[pl.ds(row, 8), lanes] = jnp.where(y_even, low, high)

    def one_slot(slot, carry):
        for half in range(2):
            faces(
                lambda j: last_ref[slot, 0, 8 * half : 8 * half + 8, j * LANES : (j + 1) * LANES],
                pl.multiple_of(slot * RHS + 8 * half, 8),
            )
        return carry

    lax.fori_loop(0, CAP, one_slot, 0)
    faces(lambda j: kap_ref[:, j * LANES : (j + 1) * LANES], CAP * RHS)
    copies[4].wait()


def add_block(slot, block, high_ref, low_ref, table_ref, weight_ref, out_ref, rows):
    at = slice(slot * PS * rows, (slot + 1) * PS * rows)
    lanes = slice(block * 256, (block + 1) * 256)
    table = table_ref[:, lanes]
    mixed = jnp.dot(high_ref[at, :], table, preferred_element_type=F32) + jnp.dot(
        low_ref[at, :], table, preferred_element_type=F32
    )
    weight = weight_ref[slot * PS : (slot + 1) * PS, lanes]
    total = out_ref[:, lanes]
    for plane in range(PS):
        total = total + weight[plane : plane + 1] * mixed[plane * rows : (plane + 1) * rows]
    out_ref[:, lanes] = total


def pair_kernel(
    old_ref, last_ref, signs_ref, table_ref, weight_ref, high_ref, low_ref, part_ref
):
    def prepare(slot, place, ref, planes):
        flips = (1 - 2 * signs_ref[slot]).astype(F32)
        for plane in planes:
            lanes = slice(plane * FACE, (plane + 1) * FACE)
            high, low = split(ref[slot, 0, :, lanes] * flips[:, lanes])
            row = (slot * PS + plane) * 32 + RHS * place
            high_ref[row : row + RHS, :] = high
            low_ref[row : row + RHS, :] = low

    part_ref[...] = jnp.zeros_like(part_ref)
    for slot in range(CAP + 1):
        for block in range(8):
            if slot < CAP:
                for place, ref in ((0, old_ref), (1, last_ref)):
                    prepare(slot, place, ref, (2 * block, 2 * block + 1))
            if 0 < slot <= EARLY:
                add_block(
                    slot - 1, block, high_ref, low_ref, table_ref, weight_ref, part_ref, 2 * RHS
                )


def operator_kernel(
    counts_ref, last_ref, coef_ref, signs_ref, xeven_ref, xodd_ref, yeven_ref, yodd_ref,
    table_ref, weight_ref, pair_high_ref, pair_low_ref, pair_part_ref,
    image_ref, message_ref, gram_ref,
    kap_ref, coupling_ref, high_ref, low_ref, part_ref, sum_ref, xlo_ref, xhi_ref, ylo_ref, yhi_ref,
):
    held = held_of(counts_ref)
    x_even = lax.axis_index("px") % 2 == 0
    y_even = lax.axis_index("py") % 2 == 0
    xlo_ref[...] = jnp.where(x_even, xodd_ref[...], xeven_ref[...])
    xhi_ref[...] = jnp.where(x_even, xeven_ref[...], xodd_ref[...])
    ylo_ref[...] = jnp.where(y_even, yodd_ref[...], yeven_ref[...])
    yhi_ref[...] = jnp.where(y_even, yeven_ref[...], yodd_ref[...])
    lane = iota((8, LANES), 1)
    row = iota((8, LANES), 0)
    kap_ref[...] = jnp.zeros_like(kap_ref)
    for slot in range(CAP):
        kap_ref[slot : slot + 1, :] = coef_ref[slot]

    def kap(j):
        return kap_ref[:, j * LANES : (j + 1) * LANES]

    def low_run(j, here, before, ghost):
        moved = lane_roll(here, PS)
        other = lane_roll(ghost, -PS * ((j // 2) % 8)) if j % 2 == 0 else lane_roll(before, PS)
        return jnp.where(lane < PS, other, moved)

    def high_run(j, here, after, ghost):
        moved = lane_roll(here, -PS)
        other = (
            lane_roll(ghost, LANES - PS - PS * ((j // 2) % 8))
            if j % 2 == 1
            else lane_roll(after, -PS)
        )
        return jnp.where(lane >= LANES - PS, other, moved)

    first = lane % PS == 0
    final = lane % PS == PS - 1
    for j in range(32):
        here = kap(j)
        col = slice((j // 16) * LANES, (j // 16 + 1) * LANES)
        end = slice((j % 2) * LANES, (j % 2 + 1) * LANES)
        if j >= 2:
            below = kap(j - 2)
        else:
            ghost = jnp.broadcast_to(xlo_ref[RHS : RHS + 1, end], (8, LANES))
            below = jnp.where(row == 0, ghost, pltpu.roll(kap(j + 30), 1, 0))
        if j < 30:
            above = kap(j + 2)
        else:
            ghost = jnp.broadcast_to(xhi_ref[RHS : RHS + 1, end], (8, LANES))
            above = jnp.where(row == held - 1, ghost, pltpu.roll(kap(j - 30), 7, 0))
        y_low = low_run(j, here, kap(j - 1) if j % 2 else None, ylo_ref[CAP * RHS :, col])
        y_high = high_run(j, here, None if j % 2 else kap(j + 1), yhi_ref[CAP * RHS :, col])
        z_low = jnp.where(first, 0.0, lane_roll(here, 1))
        z_high = jnp.where(final, 0.0, lane_roll(here, -1))
        weights = [0.5 * (here + near) for near in (below, above, y_low, y_high, z_low, z_high)]
        diagonal = functools.reduce(lambda a, b: a + b, weights)
        weights[4] = jnp.where(first, 0.0, weights[4])
        weights[5] = jnp.where(final, 0.0, weights[5])
        for place, value in enumerate(weights + [diagonal]):
            coupling_ref[place, j, 0:8, :] = value

    gram_ref[...] = jnp.zeros_like(gram_ref)
    part_ref[...] = jnp.zeros_like(part_ref)
    sum_ref[...] = pair_part_ref[...]
    contract = functools.partial(
        lax.dot_general,
        dimension_numbers=(((1,), (1,)), ((), ())),
        preferred_element_type=F32,
    )

    def stencil(slot, j):
        live = (slot < held).astype(F32)
        lanes = slice(j * LANES, (j + 1) * LANES)
        col = slice((j // 16) * LANES, (j // 16 + 1) * LANES)
        end = slice((j % 2) * LANES, (j % 2 + 1) * LANES)
        coupling = [
            jnp.broadcast_to(coupling_ref[place, j, slot : slot + 1, :], (8, LANES))
            for place in range(7)
        ]
        for half in range(2):
            rows = slice(8 * half, 8 * half + 8)

            def cells(s, k):
                return last_ref[s, 0, rows, k * LANES : (k + 1) * LANES]

            ghost_rows = slice(slot * RHS + 8 * half, slot * RHS + 8 * half + 8)
            here = cells(slot, j)
            if j >= 2:
                below = cells(slot, j - 2)
            else:
                below = cells(slot - 1, j + 30) if slot else xlo_ref[rows, end]
            if j < 30:
                above = cells(slot, j + 2)
            else:
                above = xhi_ref[rows, end]
                if slot < CAP - 1:
                    above = jnp.where(slot == held - 1, above, cells(slot + 1, j - 30))
            y_low = low_run(
                j, here, cells(slot, j - 1) if j % 2 else None, ylo_ref[ghost_rows, col]
            )
            y_high = high_run(
                j, here, None if j % 2 else cells(slot, j + 1), yhi_ref[ghost_rows, col]
            )
            near = (below, above, y_low, y_high, lane_roll(here, 1), lane_roll(here, -1))
            value = coupling[6] * here
            for weight, neighbour in zip(coupling, near):
                value = value - weight * neighbour
            image_ref[slot, 0, rows, lanes] = value * live

    def finish(slot, plane, flips):
        lanes = slice(plane * FACE, (plane + 1) * FACE)
        high, low = split(image_ref[slot, 0, :, lanes] * flips[:, lanes])
        at = slice((slot * PS + plane) * RHS, (slot * PS + plane + 1) * RHS)
        high_ref[at, :] = high
        low_ref[at, :] = low
        pair_at = slice((slot * PS + plane) * 32, (slot * PS + plane + 1) * 32)
        pair_high = pair_high_ref[pair_at, :]
        return (
            contract(pair_high, high)
            + contract(pair_high, low)
            + contract(pair_low_ref[pair_at, :], high)
        )

    for slot in range(CAP + 1):
        if slot < CAP:
            flips = (1 - 2 * signs_ref[slot]).astype(F32)
            gram = gram_ref[:, 0:RHS]
        for block in range(8):
            if slot < CAP:
                for j in range(4 * block, 4 * block + 4):
                    stencil(slot, j)
                for plane in (2 * block, 2 * block + 1):
                    gram = gram + finish(slot, plane, flips)
            if slot:
                add_block(
                    slot - 1, block, high_ref, low_ref, table_ref, weight_ref, part_ref, RHS
                )
            if slot < CAP - EARLY:
                add_block(
                    EARLY + slot, block, pair_high_ref, pair_low_ref, table_ref, weight_ref,
                    sum_ref, 2 * RHS,
                )
        if slot < CAP:
            gram_ref[:, 0:RHS] = gram
    for col in range(K // LANES):
        lanes = slice(col * LANES, (col + 1) * LANES)
        for tile in range(3):
            if tile == 0:
                top, bottom = sum_ref[0:8, lanes], sum_ref[24:32, lanes]
            else:
                top = sum_ref[8 * tile : 8 * tile + 8, lanes]
                bottom = part_ref[8 * tile - 8 : 8 * tile, lanes]
            rows = slice(8 * tile, 8 * tile + 8)
            message_ref[2 * col, rows, :] = jnp.where(lane < 64, top, lane_roll(bottom, 64))
            message_ref[2 * col + 1, rows, :] = jnp.where(lane < 64, lane_roll(top, 64), bottom)


def sum_kernel(parts_ref, gram_ref, out_ref):
    total = parts_ref[0]
    for source in range(1, GROUP):
        total = total + parts_ref[source]
    gram = gram_ref[0:8, :]
    for tile in range(1, 4):
        gram = gram + lane_roll(gram_ref[8 * tile : 8 * tile + 8, :], RHS * tile)
    for target in range(N_Z):
        out_ref[target, 0:24, :] = total
        out_ref[target, 24:32, :] = gram


def gram_kernel(parts_ref, previous_ref, residual_ref, out_ref, sketch_ref):
    summed = parts_ref[0]
    for source in range(1, N_Z):
        summed = summed + parts_ref[source]
    sketch = jnp.concatenate([summed[0:24, 0:64], summed[0:24, 64:128]], axis=0)
    sketch_ref[...] = sketch
    contract = functools.partial(
        lax.dot_general, precision=highest, preferred_element_type=F32
    )
    first = contract(previous_ref[...], sketch[0:32], dimension_numbers=(((1,), (0,)), ((), ())))
    target = contract(residual_ref[...], sketch[0:16], dimension_numbers=(((0,), (0,)), ((), ())))
    images = jnp.concatenate([first, sketch[32:48]], axis=0)
    whole = jnp.concatenate([images, target], axis=0)
    gram = contract(images, whole, dimension_numbers=(((1,), (1,)), ((), ())))
    product = jnp.concatenate(
        [lane_roll(summed[24:32], -RHS * tile)[:, 0:RHS] for tile in range(4)], axis=0
    )
    piece = jnp.concatenate([gram, product], axis=1)
    piece = jnp.concatenate([piece[0:16], piece[16:32]], axis=1)
    for target_index in range(GROUP):
        out_ref[target_index] = piece


def final_kernel(
    counts_ref, parts_ref, rows_ref, signs_ref, high_ref, low_ref, image_ref,
    new_hbm, sketch_ref, solution_ref, new_ref, sems,
):
    held = held_of(counts_ref)
    total = parts_ref[0]
    for source in range(1, GROUP):
        total = total + parts_ref[source]
    matrix = jnp.concatenate([total[:, 0:64], total[:, 64:128]], axis=0)
    projection = (matrix[:, 48:64] * (1.0 / NC)).T
    system = jnp.concatenate([matrix, jnp.zeros((32, 64), F32)], axis=1)
    row_ids = iota((32, LANES), 0)
    large, small = split(projection)
    both = jnp.concatenate([large, small], axis=0)
    copies = []
    step = 0
    for slot in range(CAP):
        flips = (1 - 2 * signs_ref[slot]).astype(F32)
        for plane in range(PS):
            lanes = slice(plane * FACE, (plane + 1) * FACE)
            at = slice((slot * PS + plane) * 32, (slot * PS + plane + 1) * 32)
            mixed = jnp.dot(both, high_ref[at, :], preferred_element_type=F32)
            mixed_low = jnp.dot(large, low_ref[at, :], preferred_element_type=F32)
            change = (mixed[0:RHS] + mixed[RHS:] + mixed_low) * flips[:, lanes]
            new = image_ref[slot, 0, :, lanes] - change
            new_ref[slot, 0, :, lanes] = jnp.where(slot < held, new, 0.0)
            if plane % 3 == 0 and step < 32:
                pivot = system[step : step + 1, :]
                scaled = pivot / pivot[:, step : step + 1]
                reduced = system - system[:, step : step + 1] * scaled
                system = jnp.where(row_ids == step, scaled, reduced)
                step += 1
        copies.append(pltpu.make_async_copy(new_ref.at[slot], new_hbm.at[slot], sems.at[slot]))
        copies[-1].start()
    solution_ref[...] = system.T[32:48, :]
    sketch = rows_ref[...]
    newer = sketch[32:48] - jnp.dot(
        projection, sketch[0:32], precision=highest, preferred_element_type=F32
    )
    whole = jnp.concatenate([sketch[0:32], newer], axis=0)
    whole = jnp.concatenate([whole, jnp.zeros_like(whole)], axis=1)
    z_index = lax.axis_index("px") // (N_PX // N_Z)
    moved = pltpu.roll(whole, LANES - z_index * SHARE, 1)
    sketch_ref[...] = moved.T[0:SHARE, :]
    for copy in copies:
        copy.wait()


def call(kernel, out_shapes, name, smem=(), scratch=(), near_in=(), near_out=(), far_in=(), far_out=()):
    def run(*args):
        args = [
            pltpu.with_memory_space_constraint(value, pltpu.VMEM if i in near_in else pltpu.HBM)
            if i in near_in or i in far_in
            else value
            for i, value in enumerate(args)
        ]
        specs = [
            pl.BlockSpec(
                memory_space=pltpu.SMEM if i in smem else pltpu.HBM if i in far_in else pltpu.VMEM
            )
            for i in range(len(args))
        ]
        return pl.pallas_call(
            kernel,
            out_shape=[
                (pltpu.VMEM if i in near_out else jax.ShapeDtypeStruct)(shape, kind)
                for i, (shape, kind) in enumerate(out_shapes)
            ],
            in_specs=specs,
            out_specs=[
                pl.BlockSpec(memory_space=pltpu.HBM if i in far_out else pltpu.VMEM)
                for i in range(len(out_shapes))
            ],
            scratch_shapes=list(scratch),
            compiler_params=pltpu.CompilerParams(vmem_limit_bytes=24 << 20),
            name=name,
        )(*args)

    return run


def partner(index, first, size):
    other = index + 1 if index % 2 == first else index - 1
    return other if 0 <= other < size else None


def px_pairs(first):
    return [
        (px * N_PY + py, partner(px, first, N_PX) * N_PY + py)
        for px in range(N_PX)
        for py in range(N_PY)
        if partner(px, first, N_PX) is not None
    ]


def py_pairs(first):
    return [
        (px * N_PY + py, px * N_PY + partner(py, first, N_PY))
        for px in range(N_PX)
        for py in range(N_PY)
        if partner(py, first, N_PY) is not None
    ]


def exchange(values, along_z=False):
    groups = [[plane * GROUP + i for i in range(GROUP)] for plane in range(N_Z)]
    if along_z:
        groups = [list(members) for members in zip(*groups)]
    return lax.all_to_all(values, AXES, 0, 0, axis_index_groups=groups, tiled=True)


def body(
    counts, coefficient, signs, basis_old, basis_last, residual_factor, previous_coef, sample_rows
):
    *faces, table, weight, last, old = call(
        pack_kernel,
        [((RHS + 8, FACE), F32)] * 2
        + [((CAP * RHS + 8, FACE), F32)] * 2
        + [((FACE, K), BF16), ((CAP * PS, K), F32)]
        + [((CAP, 1, RHS, CELLS), F32)] * 2,
        "pack",
        far_in=range(5),
        near_out=(4, 5, 6, 7),
        scratch=[
            pltpu.SMEM((N_PX,), jnp.int32),
            pltpu.VMEM((K // LANES, LANES), jnp.int32),
            pltpu.VMEM((CAP, 1, CELLS), F32),
            pltpu.VMEM((8, CELLS), F32),
            pltpu.SemaphoreType.DMA((5,)),
        ],
    )(counts, sample_rows.reshape(K // LANES, LANES), coefficient, basis_last, basis_old)
    ghosts = [
        lax.ppermute(face, AXES, pairs)
        for face, pairs in zip(faces, (px_pairs(0), px_pairs(1), py_pairs(0), py_pairs(1)))
    ]

    pair_high, pair_low, pair_part = call(
        pair_kernel,
        [
            ((CAP * PS * 32, FACE), BF16),
            ((CAP * PS * 32, FACE), BF16),
            ((32, K), F32),
        ],
        "pair",
        near_in=range(5),
        near_out=range(3),
    )(old, last, signs, table, weight)

    image, message, gram = call(
        operator_kernel,
        [
            ((CAP, 1, RHS, CELLS), F32),
            ((GROUP, 24, LANES), F32),
            ((32, LANES), F32),
        ],
        "operator",
        smem=(0,),
        near_in=(1, 4, 5, 6, 7, 8, 9, 10, 11, 12),
        near_out=(0, 2),
        scratch=[
            pltpu.VMEM((8, CELLS), F32),
            pltpu.VMEM((7, 32, 8, LANES), F32),
            pltpu.VMEM((CAP * PS * RHS, FACE), BF16),
            pltpu.VMEM((CAP * PS * RHS, FACE), BF16),
            pltpu.VMEM((RHS, K), F32),
            pltpu.VMEM((2 * RHS, K), F32),
        ]
        + [pltpu.VMEM((RHS + 8, FACE), F32)] * 2
        + [pltpu.VMEM((CAP * RHS + 8, FACE), F32)] * 2,
    )(
        counts, last, coefficient, signs, *ghosts, table, weight, pair_high, pair_low, pair_part,
    )

    (summed,) = call(sum_kernel, [((N_Z, 32, LANES), F32)], "sum", near_in=(0, 1))(exchange(message), gram)
    pieces, chunk = call(
        gram_kernel, [((GROUP, 16, LANES), F32), ((48, 64), F32)], "gram", near_in=(0,), near_out=(1,)
    )(exchange(summed, along_z=True), previous_coef.T, residual_factor)
    new_block, sketch, answer = call(
        final_kernel,
        [
            ((CAP, 1, RHS, CELLS), F32),
            ((SHARE, 48), F32),
            ((16, 32), F32),
        ],
        "final",
        smem=(0,),
        near_in=(1, 2, 3, 4, 5, 6),
        far_out=(0,),
        scratch=[pltpu.VMEM((CAP, 1, RHS, CELLS), F32), pltpu.SemaphoreType.DMA((CAP,))],
    )(counts, exchange(pieces), chunk, signs, pair_high, pair_low, image)
    return (new_block, sketch.T, answer.T)


def solution(mesh):
    in_specs = (
        P(),
        P("px", "py", None),
        P("px", "py", None),
        P("px", "py", None, None),
        P("px", "py", None, None),
        P(),
        P(),
        P(),
    )
    out_specs = (P("px", "py", None, None), P(None, ("px", "py")), P())
    return jax.shard_map(body, mesh=mesh, in_specs=in_specs, out_specs=out_specs, check_vma=False)
```

```python
import functools
import math

import jax
import jax.numpy as jnp
from jax import lax
from jax.experimental import pallas as pl
from jax.experimental.pallas import tpu as pltpu
from jax.sharding import PartitionSpec as P

PS = 16
RHS = 16
K = 2048
CAP = 6
CELLS = 4096
NC = 2097152
FACE = PS * PS
LANES = 128
N_PX = 32
N_PY = 8
N_Z = 8
GROUP = 32
EARLY = 4
SHARE = K // (N_PX * N_PY)
AXES = ("px", "py")

F32 = jnp.float32
BF16 = jnp.bfloat16
highest = lax.Precision.HIGHEST


def iota(shape, dim):
    return lax.broadcasted_iota(jnp.int32, shape, dim)


def sign_of(bits):
    for amount in (8, 4, 2, 1):
        bits = bits ^ (bits >> amount)
    return (1 - 2 * (bits & 1)).astype(F32)


def split(values):
    high = values.astype(BF16)
    return high, (values - high.astype(F32)).astype(BF16)


def lane_roll(tile, shift):
    shift = shift % LANES
    return pltpu.roll(tile, shift, 1) if shift else tile


def held_of(counts_ref):
    return counts_ref[lax.axis_index("px")]


def offset_of(counts_ref):
    index = lax.axis_index("px")
    return lax.fori_loop(
        0, N_PX, lambda i, total: total + jnp.where(i < index, counts_ref[i], 0), jnp.int32(0)
    )


def permuted(rows_ref):
    group = iota((8, LANES), 1) // SHARE
    tiles = []
    for col in range(16):
        tile = jnp.zeros((8, LANES), jnp.int32)
        for z in range(N_Z):
            here = jnp.broadcast_to(rows_ref[2 * z + col // 8 : 2 * z + col // 8 + 1, :], (8, LANES))
            base = 16 * (col % 8)
            tile = jnp.where(group == z, lane_roll(here, SHARE * z - base), tile)
            tile = jnp.where(group == N_Z + z, lane_roll(here, 64 + SHARE * z - base - 8), tile)
        tiles.append(tile[0:1])
    return jnp.concatenate(tiles, axis=1)


def make_tables(counts_ref, held, rows_ref, table_ref, weight_ref):
    offset = offset_of(counts_ref)
    rows = permuted(rows_ref)
    index = iota((16, K), 0)
    inner = sign_of(index & (rows & 15))
    outer = sign_of(index & ((rows >> 4) & 15))
    for step in range(16):
        table_ref[16 * step : 16 * step + 16, :] = (inner * outer[step : step + 1]).astype(BF16)
    plane_sign = sign_of(index & ((rows >> 8) & 15))
    slot_ids = iota((8, K), 0)
    patch = (offset + slot_ids) * N_PY + lax.axis_index("py")
    slot_sign = sign_of(patch & (rows >> 12)) * jnp.where(
        slot_ids < held, 1.0 / math.sqrt(NC), 0.0
    )
    for slot in range(CAP):
        weight_ref[slot * PS : (slot + 1) * PS, :] = plane_sign * slot_sign[slot : slot + 1]


def pack_kernel(
    counts_hbm, rows_hbm, coef_hbm, last_hbm, old_hbm,
    xeven_ref, xodd_ref, yeven_ref, yodd_ref, table_ref, weight_ref, last_ref, old_ref,
    counts_ref, rows_ref, coef_ref, kap_ref, sems,
):
    copies = [
        pltpu.make_async_copy(source, target, sems.at[i])
        for i, (source, target) in enumerate(
            (
                (counts_hbm, counts_ref), (rows_hbm, rows_ref), (coef_hbm, coef_ref),
                (last_hbm, last_ref), (old_hbm, old_ref),
            )
        )
    ]
    for copy in copies:
        copy.start()
    copies[0].wait()
    copies[1].wait()
    held = held_of(counts_ref)
    make_tables(counts_ref, held, rows_ref, table_ref, weight_ref)
    copies[2].wait()
    copies[3].wait()
    x_even = lax.axis_index("px") % 2 == 0
    y_even = lax.axis_index("py") % 2 == 0
    kap_ref[...] = jnp.zeros_like(kap_ref)
    for slot in range(CAP):
        kap_ref[slot : slot + 1, :] = coef_ref[slot]
    low = last_ref[0, 0, :, 0:FACE]
    high = last_ref[held - 1, 0, :, CELLS - FACE : CELLS]
    xeven_ref[0:RHS, :] = jnp.where(x_even, high, low)
    xodd_ref[0:RHS, :] = jnp.where(x_even, low, high)
    low = jnp.broadcast_to(kap_ref[0:1, 0:FACE], (8, FACE))
    high = jnp.broadcast_to(coef_ref[held - 1, :, CELLS - FACE : CELLS], (8, FACE))
    xeven_ref[RHS : RHS + 8, :] = jnp.where(x_even, high, low)
    xodd_ref[RHS : RHS + 8, :] = jnp.where(x_even, low, high)
    run = iota((8, LANES), 1) // PS

    def faces(read, row):
        for col in range(2):
            low = jnp.zeros((8, LANES), F32)
            high = jnp.zeros((8, LANES), F32)
            for step in range(8):
                plane = col * 8 + step
                low = jnp.where(run == step, lane_roll(read(2 * plane), PS * step), low)
                high = jnp.where(run == step, lane_roll(read(2 * plane + 1), PS * step + PS), high)
            lanes = slice(col * LANES, (col + 1) * LANES)
            yeven_ref[pl.ds(row, 8), lanes] = jnp.where(y_even, high, low)
            yodd_ref[pl.ds(row, 8), lanes] = jnp.where(y_even, low, high)

    def one_slot(slot, carry):
        for half in range(2):
            faces(
                lambda j: last_ref[slot, 0, 8 * half : 8 * half + 8, j * LANES : (j + 1) * LANES],
                pl.multiple_of(slot * RHS + 8 * half, 8),
            )
        return carry

    lax.fori_loop(0, CAP, one_slot, 0)
    faces(lambda j: kap_ref[:, j * LANES : (j + 1) * LANES], CAP * RHS)
    copies[4].wait()


def add_block(slot, block, high_ref, low_ref, table_ref, weight_ref, out_ref, rows):
    at = slice(slot * PS * rows, (slot + 1) * PS * rows)
    lanes = slice(block * 256, (block + 1) * 256)
    table = table_ref[:, lanes]
    mixed = jnp.dot(high_ref[at, :], table, preferred_element_type=F32) + jnp.dot(
        low_ref[at, :], table, preferred_element_type=F32
    )
    weight = weight_ref[slot * PS : (slot + 1) * PS, lanes]
    total = out_ref[:, lanes]
    for plane in range(PS):
        total = total + weight[plane : plane + 1] * mixed[plane * rows : (plane + 1) * rows]
    out_ref[:, lanes] = total


def pair_kernel(
    old_ref, last_ref, signs_ref, table_ref, weight_ref, high_ref, low_ref, part_ref
):
    def prepare(slot, place, ref, planes):
        flips = (1 - 2 * signs_ref[slot]).astype(F32)
        for plane in planes:
            lanes = slice(plane * FACE, (plane + 1) * FACE)
            high, low = split(ref[slot, 0, :, lanes] * flips[:, lanes])
            row = (slot * PS + plane) * 32 + RHS * place
            high_ref[row : row + RHS, :] = high
            low_ref[row : row + RHS, :] = low

    part_ref[...] = jnp.zeros_like(part_ref)
    for slot in range(CAP + 1):
        for block in range(8):
            if slot < CAP:
                for place, ref in ((0, old_ref), (1, last_ref)):
                    prepare(slot, place, ref, (2 * block, 2 * block + 1))
            if 0 < slot <= EARLY:
                add_block(
                    slot - 1, block, high_ref, low_ref, table_ref, weight_ref, part_ref, 2 * RHS
                )


def operator_kernel(
    counts_ref, last_ref, coef_ref, signs_ref, xeven_ref, xodd_ref, yeven_ref, yodd_ref,
    table_ref, weight_ref, pair_high_ref, pair_low_ref, pair_part_ref,
    image_ref, message_ref, gram_ref,
    kap_ref, coupling_ref, high_ref, low_ref, part_ref, sum_ref, xlo_ref, xhi_ref, ylo_ref, yhi_ref,
):
    held = held_of(counts_ref)
    x_even = lax.axis_index("px") % 2 == 0
    y_even = lax.axis_index("py") % 2 == 0
    xlo_ref[...] = jnp.where(x_even, xodd_ref[...], xeven_ref[...])
    xhi_ref[...] = jnp.where(x_even, xeven_ref[...], xodd_ref[...])
    ylo_ref[...] = jnp.where(y_even, yodd_ref[...], yeven_ref[...])
    yhi_ref[...] = jnp.where(y_even, yeven_ref[...], yodd_ref[...])
    lane = iota((8, LANES), 1)
    row = iota((8, LANES), 0)
    kap_ref[...] = jnp.zeros_like(kap_ref)
    for slot in range(CAP):
        kap_ref[slot : slot + 1, :] = coef_ref[slot]

    def kap(j):
        return kap_ref[:, j * LANES : (j + 1) * LANES]

    def low_run(j, here, before, ghost):
        moved = lane_roll(here, PS)
        other = lane_roll(ghost, -PS * ((j // 2) % 8)) if j % 2 == 0 else lane_roll(before, PS)
        return jnp.where(lane < PS, other, moved)

    def high_run(j, here, after, ghost):
        moved = lane_roll(here, -PS)
        other = (
            lane_roll(ghost, LANES - PS - PS * ((j // 2) % 8))
            if j % 2 == 1
            else lane_roll(after, -PS)
        )
        return jnp.where(lane >= LANES - PS, other, moved)

    first = lane % PS == 0
    final = lane % PS == PS - 1
    for j in range(32):
        here = kap(j)
        col = slice((j // 16) * LANES, (j // 16 + 1) * LANES)
        end = slice((j % 2) * LANES, (j % 2 + 1) * LANES)
        if j >= 2:
            below = kap(j - 2)
        else:
            ghost = jnp.broadcast_to(xlo_ref[RHS : RHS + 1, end], (8, LANES))
            below = jnp.where(row == 0, ghost, pltpu.roll(kap(j + 30), 1, 0))
        if j < 30:
            above = kap(j + 2)
        else:
            ghost = jnp.broadcast_to(xhi_ref[RHS : RHS + 1, end], (8, LANES))
            above = jnp.where(row == held - 1, ghost, pltpu.roll(kap(j - 30), 7, 0))
        y_low = low_run(j, here, kap(j - 1) if j % 2 else None, ylo_ref[CAP * RHS :, col])
        y_high = high_run(j, here, None if j % 2 else kap(j + 1), yhi_ref[CAP * RHS :, col])
        z_low = jnp.where(first, 0.0, lane_roll(here, 1))
        z_high = jnp.where(final, 0.0, lane_roll(here, -1))
        weights = [0.5 * (here + near) for near in (below, above, y_low, y_high, z_low, z_high)]
        diagonal = functools.reduce(lambda a, b: a + b, weights)
        weights[4] = jnp.where(first, 0.0, weights[4])
        weights[5] = jnp.where(final, 0.0, weights[5])
        for place, value in enumerate(weights + [diagonal]):
            coupling_ref[place, j, 0:8, :] = value

    gram_ref[...] = jnp.zeros_like(gram_ref)
    part_ref[...] = jnp.zeros_like(part_ref)
    sum_ref[...] = pair_part_ref[...]
    contract = functools.partial(
        lax.dot_general,
        dimension_numbers=(((1,), (1,)), ((), ())),
        preferred_element_type=F32,
    )

    def stencil(slot, j):
        live = (slot < held).astype(F32)
        lanes = slice(j * LANES, (j + 1) * LANES)
        col = slice((j // 16) * LANES, (j // 16 + 1) * LANES)
        end = slice((j % 2) * LANES, (j % 2 + 1) * LANES)
        coupling = [
            jnp.broadcast_to(coupling_ref[place, j, slot : slot + 1, :], (8, LANES))
            for place in range(7)
        ]
        for half in range(2):
            rows = slice(8 * half, 8 * half + 8)

            def cells(s, k):
                return last_ref[s, 0, rows, k * LANES : (k + 1) * LANES]

            ghost_rows = slice(slot * RHS + 8 * half, slot * RHS + 8 * half + 8)
            here = cells(slot, j)
            if j >= 2:
                below = cells(slot, j - 2)
            else:
                below = cells(slot - 1, j + 30) if slot else xlo_ref[rows, end]
            if j < 30:
                above = cells(slot, j + 2)
            else:
                above = xhi_ref[rows, end]
                if slot < CAP - 1:
                    above = jnp.where(slot == held - 1, above, cells(slot + 1, j - 30))
            y_low = low_run(
                j, here, cells(slot, j - 1) if j % 2 else None, ylo_ref[ghost_rows, col]
            )
            y_high = high_run(
                j, here, None if j % 2 else cells(slot, j + 1), yhi_ref[ghost_rows, col]
            )
            near = (below, above, y_low, y_high, lane_roll(here, 1), lane_roll(here, -1))
            value = coupling[6] * here
            for weight, neighbour in zip(coupling, near):
                value = value - weight * neighbour
            image_ref[slot, 0, rows, lanes] = value * live

    def finish(slot, plane, flips):
        lanes = slice(plane * FACE, (plane + 1) * FACE)
        high, low = split(image_ref[slot, 0, :, lanes] * flips[:, lanes])
        at = slice((slot * PS + plane) * RHS, (slot * PS + plane + 1) * RHS)
        high_ref[at, :] = high
        low_ref[at, :] = low
        pair_at = slice((slot * PS + plane) * 32, (slot * PS + plane + 1) * 32)
        pair_high = pair_high_ref[pair_at, :]
        return (
            contract(pair_high, high)
            + contract(pair_high, low)
            + contract(pair_low_ref[pair_at, :], high)
        )

    for slot in range(CAP + 1):
        if slot < CAP:
            flips = (1 - 2 * signs_ref[slot]).astype(F32)
            gram = gram_ref[:, 0:RHS]
        for block in range(8):
            if slot < CAP:
                for j in range(4 * block, 4 * block + 4):
                    stencil(slot, j)
                for plane in (2 * block, 2 * block + 1):
                    gram = gram + finish(slot, plane, flips)
            if slot:
                add_block(
                    slot - 1, block, high_ref, low_ref, table_ref, weight_ref, part_ref, RHS
                )
            if slot < CAP - EARLY:
                add_block(
                    EARLY + slot, block, pair_high_ref, pair_low_ref, table_ref, weight_ref,
                    sum_ref, 2 * RHS,
                )
        if slot < CAP:
            gram_ref[:, 0:RHS] = gram
    for col in range(K // LANES):
        lanes = slice(col * LANES, (col + 1) * LANES)
        for tile in range(3):
            if tile == 0:
                top, bottom = sum_ref[0:8, lanes], sum_ref[24:32, lanes]
            else:
                top = sum_ref[8 * tile : 8 * tile + 8, lanes]
                bottom = part_ref[8 * tile - 8 : 8 * tile, lanes]
            rows = slice(8 * tile, 8 * tile + 8)
            message_ref[2 * col, rows, :] = jnp.where(lane < 64, top, lane_roll(bottom, 64))
            message_ref[2 * col + 1, rows, :] = jnp.where(lane < 64, lane_roll(top, 64), bottom)


def sum_kernel(parts_ref, gram_ref, out_ref):
    total = parts_ref[0]
    for source in range(1, GROUP):
        total = total + parts_ref[source]
    gram = gram_ref[0:8, :]
    for tile in range(1, 4):
        gram = gram + lane_roll(gram_ref[8 * tile : 8 * tile + 8, :], RHS * tile)
    for target in range(N_Z):
        out_ref[target, 0:24, :] = total
        out_ref[target, 24:32, :] = gram


def gram_kernel(parts_ref, previous_ref, residual_ref, out_ref, sketch_ref):
    summed = parts_ref[0]
    for source in range(1, N_Z):
        summed = summed + parts_ref[source]
    sketch = jnp.concatenate([summed[0:24, 0:64], summed[0:24, 64:128]], axis=0)
    sketch_ref[...] = sketch
    contract = functools.partial(
        lax.dot_general, precision=highest, preferred_element_type=F32
    )
    first = contract(previous_ref[...], sketch[0:32], dimension_numbers=(((1,), (0,)), ((), ())))
    target = contract(residual_ref[...], sketch[0:16], dimension_numbers=(((0,), (0,)), ((), ())))
    images = jnp.concatenate([first, sketch[32:48]], axis=0)
    whole = jnp.concatenate([images, target], axis=0)
    gram = contract(images, whole, dimension_numbers=(((1,), (1,)), ((), ())))
    product = jnp.concatenate(
        [lane_roll(summed[24:32], -RHS * tile)[:, 0:RHS] for tile in range(4)], axis=0
    )
    piece = jnp.concatenate([gram, product], axis=1)
    piece = jnp.concatenate([piece[0:16], piece[16:32]], axis=1)
    for target_index in range(GROUP):
        out_ref[target_index] = piece


def eliminate(system, step, row_ids):
    first = jnp.broadcast_to(system[:, step : step + 1], (32, LANES))
    second = jnp.broadcast_to(system[:, step + 1 : step + 2], (32, LANES))
    top, bottom = system[step : step + 1, :], system[step + 1 : step + 2, :]
    a, b = first[step : step + 1], second[step : step + 1]
    c, d = first[step + 1 : step + 2], second[step + 1 : step + 2]
    inverse = 1.0 / a
    right, below = b * inverse, c * inverse
    last = 1.0 / (d - c * right)
    corner, side, under = inverse + right * last * below, -right * last, -below * last
    one = first * corner + second * under
    two = first * side + second * last
    is_top, is_bottom = row_ids == step, row_ids == step + 1
    one = jnp.where(is_top, -corner, jnp.where(is_bottom, -under, one))
    two = jnp.where(is_top, -side, jnp.where(is_bottom, -last, two))
    base = jnp.where(is_top | is_bottom, 0.0, system)
    return base - one * top - two * bottom


def final_kernel(
    counts_ref, parts_ref, rows_ref, signs_ref, high_ref, low_ref, image_ref,
    new_hbm, sketch_ref, solution_ref, new_ref, sems,
):
    held = held_of(counts_ref)
    total = parts_ref[0]
    for source in range(1, GROUP):
        total = total + parts_ref[source]
    matrix = jnp.concatenate([total[:, 0:64], total[:, 64:128]], axis=0)
    projection = (matrix[:, 48:64] * (1.0 / NC)).T
    system = jnp.concatenate([matrix, jnp.zeros((32, 64), F32)], axis=1)
    row_ids = iota((32, LANES), 0)
    large, small = split(projection)
    both = jnp.concatenate([large, small], axis=0)
    copies = []
    step = 0
    for slot in range(CAP):
        flips = (1 - 2 * signs_ref[slot]).astype(F32)
        for plane in range(PS):
            lanes = slice(plane * FACE, (plane + 1) * FACE)
            at = slice((slot * PS + plane) * 32, (slot * PS + plane + 1) * 32)
            mixed = jnp.dot(both, high_ref[at, :], preferred_element_type=F32)
            mixed_low = jnp.dot(large, low_ref[at, :], preferred_element_type=F32)
            change = (mixed[0:RHS] + mixed[RHS:] + mixed_low) * flips[:, lanes]
            new = image_ref[slot, 0, :, lanes] - change
            new_ref[slot, 0, :, lanes] = jnp.where(slot < held, new, 0.0)
            if plane % 6 == 0 and step < 32:
                system = eliminate(system, step, row_ids)
                step += 2
        copies.append(pltpu.make_async_copy(new_ref.at[slot], new_hbm.at[slot], sems.at[slot]))
        copies[-1].start()
    while step < 32:
        system = eliminate(system, step, row_ids)
        step += 2
    solution_ref[...] = system.T[32:48, :]
    sketch = rows_ref[...]
    newer = sketch[32:48] - jnp.dot(
        projection, sketch[0:32], precision=highest, preferred_element_type=F32
    )
    whole = jnp.concatenate([sketch[0:32], newer], axis=0)
    whole = jnp.concatenate([whole, jnp.zeros_like(whole)], axis=1)
    z_index = lax.axis_index("px") // (N_PX // N_Z)
    moved = pltpu.roll(whole, LANES - z_index * SHARE, 1)
    sketch_ref[...] = moved.T[0:SHARE, :]
    for copy in copies:
        copy.wait()


def call(kernel, out_shapes, name, smem=(), scratch=(), near_in=(), near_out=(), far_in=(), far_out=()):
    def run(*args):
        args = [
            pltpu.with_memory_space_constraint(value, pltpu.VMEM if i in near_in else pltpu.HBM)
            if i in near_in or i in far_in
            else value
            for i, value in enumerate(args)
        ]
        specs = [
            pl.BlockSpec(
                memory_space=pltpu.SMEM if i in smem else pltpu.HBM if i in far_in else pltpu.VMEM
            )
            for i in range(len(args))
        ]
        return pl.pallas_call(
            kernel,
            out_shape=[
                (pltpu.VMEM if i in near_out else jax.ShapeDtypeStruct)(shape, kind)
                for i, (shape, kind) in enumerate(out_shapes)
            ],
            in_specs=specs,
            out_specs=[
                pl.BlockSpec(memory_space=pltpu.HBM if i in far_out else pltpu.VMEM)
                for i in range(len(out_shapes))
            ],
            scratch_shapes=list(scratch),
            compiler_params=pltpu.CompilerParams(vmem_limit_bytes=24 << 20),
            name=name,
        )(*args)

    return run


def partner(index, first, size):
    other = index + 1 if index % 2 == first else index - 1
    return other if 0 <= other < size else None


def px_pairs(first):
    return [
        (px * N_PY + py, partner(px, first, N_PX) * N_PY + py)
        for px in range(N_PX)
        for py in range(N_PY)
        if partner(px, first, N_PX) is not None
    ]


def py_pairs(first):
    return [
        (px * N_PY + py, px * N_PY + partner(py, first, N_PY))
        for px in range(N_PX)
        for py in range(N_PY)
        if partner(py, first, N_PY) is not None
    ]


def exchange(values, along_z=False):
    groups = [[plane * GROUP + i for i in range(GROUP)] for plane in range(N_Z)]
    if along_z:
        groups = [list(members) for members in zip(*groups)]
    return lax.all_to_all(values, AXES, 0, 0, axis_index_groups=groups, tiled=True)


def body(
    counts, coefficient, signs, basis_old, basis_last, residual_factor, previous_coef, sample_rows
):
    *faces, table, weight, last, old = call(
        pack_kernel,
        [((RHS + 8, FACE), F32)] * 2
        + [((CAP * RHS + 8, FACE), F32)] * 2
        + [((FACE, K), BF16), ((CAP * PS, K), F32)]
        + [((CAP, 1, RHS, CELLS), F32)] * 2,
        "pack",
        far_in=range(5),
        near_out=(4, 5, 6, 7),
        scratch=[
            pltpu.SMEM((N_PX,), jnp.int32),
            pltpu.VMEM((K // LANES, LANES), jnp.int32),
            pltpu.VMEM((CAP, 1, CELLS), F32),
            pltpu.VMEM((8, CELLS), F32),
            pltpu.SemaphoreType.DMA((5,)),
        ],
    )(counts, sample_rows.reshape(K // LANES, LANES), coefficient, basis_last, basis_old)
    ghosts = [
        lax.ppermute(face, AXES, pairs)
        for face, pairs in zip(faces, (px_pairs(0), px_pairs(1), py_pairs(0), py_pairs(1)))
    ]

    pair_high, pair_low, pair_part = call(
        pair_kernel,
        [
            ((CAP * PS * 32, FACE), BF16),
            ((CAP * PS * 32, FACE), BF16),
            ((32, K), F32),
        ],
        "pair",
        near_in=range(5),
        near_out=range(3),
    )(old, last, signs, table, weight)

    image, message, gram = call(
        operator_kernel,
        [
            ((CAP, 1, RHS, CELLS), F32),
            ((GROUP, 24, LANES), F32),
            ((32, LANES), F32),
        ],
        "operator",
        smem=(0,),
        near_in=(1, 4, 5, 6, 7, 8, 9, 10, 11, 12),
        near_out=(0, 2),
        scratch=[
            pltpu.VMEM((8, CELLS), F32),
            pltpu.VMEM((7, 32, 8, LANES), F32),
            pltpu.VMEM((CAP * PS * RHS, FACE), BF16),
            pltpu.VMEM((CAP * PS * RHS, FACE), BF16),
            pltpu.VMEM((RHS, K), F32),
            pltpu.VMEM((2 * RHS, K), F32),
        ]
        + [pltpu.VMEM((RHS + 8, FACE), F32)] * 2
        + [pltpu.VMEM((CAP * RHS + 8, FACE), F32)] * 2,
    )(
        counts, last, coefficient, signs, *ghosts, table, weight, pair_high, pair_low, pair_part,
    )

    (summed,) = call(sum_kernel, [((N_Z, 32, LANES), F32)], "sum", near_in=(0, 1))(exchange(message), gram)
    pieces, chunk = call(
        gram_kernel, [((GROUP, 16, LANES), F32), ((48, 64), F32)], "gram", near_in=(0,), near_out=(1,)
    )(exchange(summed, along_z=True), previous_coef.T, residual_factor)
    new_block, sketch, answer = call(
        final_kernel,
        [
            ((CAP, 1, RHS, CELLS), F32),
            ((SHARE, 48), F32),
            ((16, 32), F32),
        ],
        "final",
        smem=(0,),
        near_in=(1, 2, 3, 4, 5, 6),
        far_out=(0,),
        scratch=[pltpu.VMEM((CAP, 1, RHS, CELLS), F32), pltpu.SemaphoreType.DMA((CAP,))],
    )(counts, exchange(pieces), chunk, signs, pair_high, pair_low, image)
    return (new_block, sketch.T, answer.T)


def solution(mesh):
    in_specs = (
        P(),
        P("px", "py", None),
        P("px", "py", None),
        P("px", "py", None, None),
        P("px", "py", None, None),
        P(),
        P(),
        P(),
    )
    out_specs = (P("px", "py", None, None), P(None, ("px", "py")), P())
    return jax.shard_map(body, mesh=mesh, in_specs=in_specs, out_specs=out_specs, check_vma=False)
```
